128 devices in a mesh: tile: 32 (over z_hi, x, y), blk: 4 (over z_lo, core).
Axes of the slice: x: 4, y: 4, z: 4 (z_hi: 2, z_lo: 2; z = z_hi * 2 + z_lo), core: 2. Of those that a mesh axis runs over, the one named last changes fastest.
Arguments:
- image_tokens: bfloat16 [16, 1024, 1536], P(None, 'tile', 'blk'), may hold values from -10 to 10
- text_tokens: bfloat16 [16, 160, 1536], P(None, 'tile', 'blk'), may hold values from -10 to 10
- step_index: int32 [16], replicated, may hold values from 0 to 27
- text_length: int32 [16], replicated, may hold values from 1 to 160, as said below
- image_table: bfloat16 [28, 6, 1536], replicated, may hold values from -3 to 3
- text_table: bfloat16 [28, 3, 1536], replicated, may hold values from -3 to 3
- qkv_image: bfloat16 [1536, 3, 1536], P(None, None, 'blk'), may hold values from -0.15625 to 0.15625
- qkv_text: bfloat16 [1536, 3, 1536], P(None, None, 'blk'), may hold values from -0.15625 to 0.15625
- attn_out_image: bfloat16 [1536, 1536], P('blk'), may hold values from -0.15625 to 0.15625
- attn_out_text: bfloat16 [1536, 1536], P('blk'), may hold values from -0.15625 to 0.15625
- query_gain_image: float32 [64], replicated, may hold values from 1 to 12
- key_gain_image: float32 [64], replicated, may hold values from 1 to 12
- query_gain_text: float32 [64], replicated, may hold values from 1 to 12
- key_gain_text: float32 [64], replicated, may hold values from 1 to 12
- up_weight: bfloat16 [1536, 6144], P(None, 'blk'), may hold values from -0.15625 to 0.15625
- down_weight: bfloat16 [6144, 1536], P('blk'), may hold values from -0.078125 to 0.078125
Outputs:
- image_out: bfloat16 [16, 1024, 1536], P(None, 'tile', 'blk')
- text_out: bfloat16 [16, 160, 1536], P(None, 'tile', 'blk')
The draws below stay inside these ranges and needn't reach their ends.
Inputs may be any that keep to these rules, and one draw needn't show every extreme that they name: `text_length`: some request has all 160 slots valid.
All inputs are finite; a program needn't handle non-finite values.
Results may differ from the reference program's by a relative error of at most 0.015.
The reference program's roundings to bfloat16 on the way (of `image_acts`, `text_acts`, `value_heads`, `weights`, `attended`, `image_mid`, `mlp_acts` and `hidden`) count: a program that leaves them out, or rounds other values in their place, can miss the bound.
Values may be sent and summed in bfloat16 or wider, within the bound.
No kernel may reach another device: no remote copies, remote signals or barrier semaphores. Data moves between devices by JAX's collectives and lax.ppermute only.
A program may use at most 192 MiB of HBM per device.

```python
import math
import jax
import jax.numpy as jnp
from jax import lax

D = 1536
HEADS = 24
HEAD_DIM = 64
FF = 6144
STEPS = 28
R = 16
IMG = 1024
TXT = 160


def draw_field(key, seq_length):
    base_key, column_key = jax.random.split(key, 2)
    values = jax.random.truncated_normal(base_key, -3.0, 3.0, (R, seq_length, D), jnp.float32)
    column_scale = 2.0 ** jax.random.uniform(column_key, (D,), jnp.float32, -1.0, 1.0)
    return values * column_scale


def draw_image_tokens(key, part):
    return draw_field(jax.random.fold_in(key, 11), IMG).astype(jnp.bfloat16)


def draw_text_tokens(key, part):
    return draw_field(jax.random.fold_in(key, 12), TXT).astype(jnp.bfloat16)


def draw_text_length(key, part):
    first_key, second_key = jax.random.split(jax.random.fold_in(key, 7))
    lengths = jax.random.randint(first_key, (R,), 1, TXT + 1)
    chosen = jax.random.randint(second_key, (), 0, R)
    return jnp.where(jnp.arange(R) == chosen, TXT, lengths).astype(jnp.int32)


def draw_gain(key):
    return jnp.exp(jax.random.uniform(key, (HEAD_DIM,), jnp.float32, 0.0, math.log(2.5)))


def draw_query_gain_image(key, part):
    return draw_gain(jax.random.fold_in(key, 21))


def draw_key_gain_image(key, part):
    return draw_gain(jax.random.fold_in(key, 22))


def draw_query_gain_text(key, part):
    return draw_gain(jax.random.fold_in(key, 23))


def draw_key_gain_text(key, part):
    return draw_gain(jax.random.fold_in(key, 24))


def place_ends(array, rng, least, high):
    shape = array.shape
    index_at = [jax.random.randint(jax.random.fold_in(rng, axis), (), 0, shape[axis]) for axis in range(len(shape))]
    array = array.at[tuple(index_at)].set(least)
    longest = shape.index(max(shape))
    index_at[longest] = (index_at[longest] + 1) % shape[longest]
    return array.at[tuple(index_at)].set(high)


def block_levels(rng, shape, cuts, low, top_value):
    level, own = 1.0, jax.random.fold_in(rng, 6)
    for dim, blocks in cuts:
        steps = jnp.exp(jax.random.uniform(jax.random.fold_in(own, dim), (blocks,), jnp.float32, low / len(cuts), top_value / len(cuts)))
        level = level * jnp.repeat(steps, shape[dim] // blocks).reshape([-1 if axis == dim else 1 for axis in range(len(shape))])
    return level


def centred(rng, dims, scale, bound, pieces=(), kind=jnp.bfloat16):
    drawn = scale * jax.random.normal(rng, dims, jnp.float32)
    if pieces:
        drawn = drawn * block_levels(rng, dims, pieces, -0.22, 0.18)
    return jnp.clip(drawn, -bound, bound).astype(kind)


def setup_inputs(seed: int = 0) -> dict:
    splits = jax.random.split(jax.random.key(seed), 17)
    image_tokens = draw_image_tokens(jax.random.fold_in(splits[16], 71), 0)
    text_tokens = draw_text_tokens(jax.random.fold_in(splits[16], 71), 0)
    step_index = place_ends(jax.random.randint(splits[2], (R,), 0, STEPS), jax.random.fold_in(splits[2], 1), 0, STEPS - 1).astype(jnp.int32)
    text_length = draw_text_length(jax.random.fold_in(splits[16], 71), 0)
    image_table = centred(splits[4], (STEPS, 6, D), 0.5, 3.0)
    text_table = centred(splits[5], (STEPS, 3, D), 0.5, 3.0)
    qkv_image = centred(splits[6], (D, 3, D), D ** -0.5, 0.15625, ((2, 4),))
    qkv_text = centred(splits[7], (D, 3, D), D ** -0.5, 0.15625, ((2, 4),))
    attn_out_image = centred(splits[8], (D, D), D ** -0.5, 0.15625, ((0, 4),))
    attn_out_text = centred(splits[9], (D, D), D ** -0.5, 0.15625, ((0, 4),))
    query_gain_image = draw_query_gain_image(jax.random.fold_in(splits[16], 71), 0)
    key_gain_image = draw_key_gain_image(jax.random.fold_in(splits[16], 71), 0)
    query_gain_text = draw_query_gain_text(jax.random.fold_in(splits[16], 71), 0)
    key_gain_text = draw_key_gain_text(jax.random.fold_in(splits[16], 71), 0)
    up_weight = centred(splits[14], (D, FF), D ** -0.5, 0.15625, ((1, 4),))
    down_weight = centred(splits[15], (FF, D), FF ** -0.5, 0.078125, ((0, 4),))
    return {"image_tokens": image_tokens, "text_tokens": text_tokens, "step_index": step_index, "text_length": text_length, "image_table": image_table, "text_table": text_table, "qkv_image": qkv_image, "qkv_text": qkv_text, "attn_out_image": attn_out_image, "attn_out_text": attn_out_text, "query_gain_image": query_gain_image, "key_gain_image": key_gain_image, "query_gain_text": query_gain_text, "key_gain_text": key_gain_text, "up_weight": up_weight, "down_weight": down_weight}


def rounded(values):
    return lax.optimization_barrier(values.astype(jnp.bfloat16))

def layer_norm(values):
    centre = lax.optimization_barrier(jnp.mean(values, axis=-1, keepdims=True))
    spread = lax.optimization_barrier(jnp.mean(jnp.square(values - centre), axis=-1, keepdims=True))
    return (values - centre) * lax.rsqrt(spread + 1e-06)

def modulate(normed, shift_rows, scale_rows):
    return rounded(normed * (1.0 + scale_rows[:, None, :]) + shift_rows[:, None, :])

def head_norm(values, gain_vector):
    inverse_rms = lax.rsqrt(lax.optimization_barrier(jnp.mean(jnp.square(values), axis=-1, keepdims=True)) + 1e-06)
    return rounded(values * inverse_rms * gain_vector)

def project_heads(activations, weight, gain_query, gain_key):
    projected = jnp.einsum('rsd,dke->rske', activations.astype(jnp.float32), weight.astype(jnp.float32))
    split_shape = projected.shape[:2] + (HEADS, HEAD_DIM)
    query_heads = head_norm(projected[:, :, 0].reshape(split_shape), gain_query)
    key_heads = head_norm(projected[:, :, 1].reshape(split_shape), gain_key)
    value_heads = rounded(projected[:, :, 2].reshape(split_shape))
    return (query_heads, key_heads, value_heads)

def attend_one(bundle):
    queries, key_heads, value_heads, length = bundle
    position = jnp.arange(IMG + TXT)
    visible = (position < IMG) | (position - IMG < length)
    scores = jnp.einsum('qhe,khe->hqk', queries.astype(jnp.float32), key_heads.astype(jnp.float32)) * HEAD_DIM ** (-0.5)
    visible_mask = visible[None, None, :]
    row_max = lax.optimization_barrier(jnp.max(jnp.where(visible_mask, scores, -1e+30), axis=-1, keepdims=True))
    weights = jnp.where(visible_mask, jnp.exp(scores - row_max), 0.0)
    row_sum = lax.optimization_barrier(jnp.sum(weights, axis=-1, keepdims=True))
    combined = jnp.einsum('hqk,khe->qhe', rounded(weights).astype(jnp.float32), value_heads.astype(jnp.float32))
    return rounded(combined / jnp.transpose(row_sum, (1, 0, 2)))

def reference(image_tokens, text_tokens, step_index, text_length, image_table, text_table, qkv_image, qkv_text, attn_out_image, attn_out_text, query_gain_image, key_gain_image, query_gain_text, key_gain_text, up_weight, down_weight):
    image_mods = image_table[step_index].astype(jnp.float32)
    text_mods = text_table[step_index].astype(jnp.float32)
    image_float = image_tokens.astype(jnp.float32)
    text_float = text_tokens.astype(jnp.float32)
    image_acts = modulate(layer_norm(image_float), image_mods[:, 0], image_mods[:, 1])
    text_acts = modulate(layer_norm(text_float), text_mods[:, 0], text_mods[:, 1])
    image_q, image_k, image_v = project_heads(image_acts, qkv_image, query_gain_image, key_gain_image)
    text_q, text_k, text_v = project_heads(text_acts, qkv_text, query_gain_text, key_gain_text)
    joint_q = jnp.concatenate([image_q, text_q], axis=1)
    joint_k = jnp.concatenate([image_k, text_k], axis=1)
    joint_v = jnp.concatenate([image_v, text_v], axis=1)
    attended = lax.map(attend_one, (joint_q, joint_k, joint_v, text_length))
    attended = attended.reshape(R, IMG + TXT, D)
    image_proj = jnp.einsum('rsd,de->rse', attended[:, :IMG].astype(jnp.float32), attn_out_image.astype(jnp.float32))
    text_proj = jnp.einsum('rsd,de->rse', attended[:, IMG:].astype(jnp.float32), attn_out_text.astype(jnp.float32))
    image_mid = rounded(image_float + image_mods[:, 2][:, None, :] * image_proj)
    text_out = (text_float + text_mods[:, 2][:, None, :] * text_proj).astype(jnp.bfloat16)
    middle_float = image_mid.astype(jnp.float32)
    mlp_acts = modulate(layer_norm(middle_float), image_mods[:, 3], image_mods[:, 4])
    hidden = rounded(jax.nn.gelu(jnp.einsum('rsd,df->rsf', mlp_acts.astype(jnp.float32), up_weight.astype(jnp.float32)), approximate=True))
    down_term = jnp.einsum('rsf,fd->rsd', hidden.astype(jnp.float32), down_weight.astype(jnp.float32))
    image_out = (middle_float + image_mods[:, 5][:, None, :] * down_term).astype(jnp.bfloat16)
    return (image_out, text_out)
```

```python
import functools

import jax
import jax.numpy as jnp
from jax import lax
from jax.experimental import pallas as pl
from jax.experimental.pallas import tpu as pltpu
from jax.sharding import PartitionSpec as P

HEAD_DIM = 64
BF = jnp.bfloat16
F32 = jnp.float32
HIDDEN_BIAS = -32768.0
TXT_PAD = 8
VMEM_LIMIT = 56 << 20


def dot(left, right):
    return jnp.dot(left, right, preferred_element_type=F32)


def dot_t(left, right):
    return lax.dot_general(left, right, (((1,), (1,)), ((), ())), preferred_element_type=F32)


def normed_acts(pieces, mods, shift_row, scale_row, width):
    total = sum(jnp.sum(piece, axis=-1, keepdims=True) for piece in pieces)
    centre = total * (1.0 / width)
    moved = [piece - centre for piece in pieces]
    spread = sum(jnp.sum(piece * piece, axis=-1, keepdims=True) for piece in moved) * (1.0 / width)
    inverse = lax.rsqrt(spread + 1e-06)
    return [
        (piece * inverse * (1.0 + mod[scale_row : scale_row + 1]) + mod[shift_row : shift_row + 1]).astype(BF)
        for piece, mod in zip(moved, mods)
    ]


def head_scale(values, group_ref):
    squares = values * values
    high = squares.astype(BF)
    low = (squares - high.astype(F32)).astype(BF)
    return lax.rsqrt(dot(high, group_ref[...]) + dot(low, group_ref[...]) + 1e-06)


def qkv_kernel(
    place_ref, x0, x1, x2, x3, imod_ref, tmod_ref, wimg_ref, wtxt_ref, gain_ref, group_ref,
    q_ref, kv_ref, acts_ref,
):
    step = pl.program_id(0)
    blk = place_ref[0]
    part = x0.shape[2]
    img_rows = x0.shape[0] * (x0.shape[1] - TXT_PAD)
    rows = x0.shape[0] * x0.shape[1]

    @pl.when(step == 0)
    def _():
        for text in (False, True):
            pieces, mods = [], []
            for j, ref in enumerate((x0, x1, x2, x3)):
                if text:
                    value = ref[:, ref.shape[1] - TXT_PAD :, :].astype(F32)
                    mods.append(tmod_ref[blk ^ j])
                else:
                    value = ref[:, : ref.shape[1] - TXT_PAD, :].astype(F32)
                    mods.append(imod_ref[blk ^ j])
                pieces.append(value.reshape(-1, part))
            acts = normed_acts(pieces, mods, 0, 1, 4 * part)
            for j in range(4):
                if text:
                    acts_ref[j, img_rows:rows, :] = acts[j]
                else:
                    acts_ref[j, :img_rows, :] = acts[j]

    def project(w_ref, start, stop):
        out = None
        for j in range(4):
            offset = pl.multiple_of((blk ^ j) * part, part)
            term = dot(acts_ref[j, start:stop, :], w_ref[0, pl.ds(offset, part), :])
            out = term if out is None else out + term
        return out

    for w_ref, start, stop, row in ((wimg_ref, 0, img_rows, 0), (wtxt_ref, img_rows, rows, 1)):
        values = project(w_ref, start, stop)

        @pl.when(step == 0)
        def _():
            kv_ref[0, start:stop, :] = (
                values * head_scale(values, group_ref) * gain_ref[2 + row : 3 + row, :]
            ).astype(BF)

        @pl.when(step == 1)
        def _():
            kv_ref[0, start:stop, :] = values.astype(BF)

        @pl.when(step == 2)
        def _():
            normed = (values * head_scale(values, group_ref) * gain_ref[row : row + 1, :]).astype(BF)
            q_ref[start:stop, :] = normed * BF(HEAD_DIM**-0.5)


def qkv_call(place, pieces, imod, tmod, wimg, wtxt, gains, group):
    sources, slot, part = pieces[0].shape
    rows = sources * slot
    width = 4 * part

    def whole(shape):
        return pl.BlockSpec(shape, lambda i, s: (0,) * len(shape))

    third = pl.BlockSpec((1, width, part), lambda i, s: ((i + 1) % 3, 0, 0))
    return pl.pallas_call(
        qkv_kernel,
        out_shape=(
            jax.ShapeDtypeStruct((rows, part), BF),
            jax.ShapeDtypeStruct((2, rows, part), BF),
        ),
        grid_spec=pltpu.PrefetchScalarGridSpec(
            num_scalar_prefetch=1,
            grid=(3,),
            in_specs=[whole(pieces[0].shape)] * 4
            + [whole(imod.shape), whole(tmod.shape), third, third, whole(gains.shape), whole(group.shape)],
            out_specs=(
                whole((rows, part)),
                pl.BlockSpec((1, rows, part), lambda i, s: (jnp.minimum(i, 1), 0, 0)),
            ),
            scratch_shapes=[pltpu.VMEM((4, rows, part), BF)],
        ),
        compiler_params=pltpu.CompilerParams(
            dimension_semantics=("arbitrary",), vmem_limit_bytes=VMEM_LIMIT
        ),
        cost_estimate=pl.CostEstimate(
            flops=2 * rows * width * part * 3, transcendentals=0, bytes_accessed=9 << 20
        ),
        name="qkv",
    )(place, *pieces, imod, tmod, wimg, wtxt, gains, group)


def key_bias(place_ref, rows, img_rows, other):
    row = lax.broadcasted_iota(jnp.int32, (rows, 128), 0)
    inner = row - img_rows
    source = inner >> 3
    slot = inner & 7
    parity = place_ref[1] ^ other
    tile = (source >> 2) * 8 + parity * 4 + (source & 3)
    seen = (inner < 0) | ((slot < 5) & (tile * 5 + slot < place_ref[2]))
    return jnp.where(seen, 0.0, HIDDEN_BIAS).astype(BF)


def attend_kernel(place_ref, q_ref, kv_ref, ko_ref, wimg_ref, wtxt_ref, out_ref, att_ref):
    blk = place_ref[0]
    rows, part = q_ref.shape
    img_rows = rows // 5 * 4
    pairs = part // 128
    lane = lax.broadcasted_iota(jnp.int32, (rows, 128), 1)
    one_lane = jnp.where(lane == 0, 1.0, 0.0).astype(BF)
    ones = jnp.ones((rows, 128), BF)
    biases = [key_bias(place_ref, rows, img_rows, other) for other in (0, 1)]
    half = rows // 2
    for pair in range(pairs):
        cols = slice(pair * 128, pair * 128 + 128)
        keys = [
            jnp.concatenate([ref[0, :, cols], bias], axis=1)
            for ref, bias in zip((kv_ref, ko_ref), biases)
        ]
        vals = [jnp.concatenate([ref[1, :, cols], ones], axis=1) for ref in (kv_ref, ko_ref)]
        query = q_ref[:, cols]
        for piece in range(2):
            span = slice(piece * half, piece * half + half)
            outs = []
            for head in range(2):
                mine = (lane[span] < 64) if head == 0 else (lane[span] >= 64)
                masked = jnp.where(mine, query[span], BF(0.0))
                left = jnp.concatenate([masked, one_lane[span]], axis=1)
                scores = [dot_t(left, key) for key in keys]
                top = jnp.maximum(
                    jnp.max(scores[0], axis=-1, keepdims=True),
                    jnp.max(scores[1], axis=-1, keepdims=True),
                )
                weights = [jnp.exp(score - top).astype(BF) for score in scores]
                both = dot(weights[0], vals[0]) + dot(weights[1], vals[1])
                outs.append(both[:, :128] / both[:, 128:])
            att_ref[span, cols] = jnp.where(lane[span] < 64, outs[0], outs[1]).astype(BF)
    for j in range(4):
        offset = pl.multiple_of((blk ^ j) * part, part)
        out_ref[j, :img_rows, :] = dot(att_ref[:img_rows, :], wimg_ref[:, pl.ds(offset, part)]).astype(BF)
        out_ref[j, img_rows:, :] = dot(att_ref[img_rows:, :], wtxt_ref[:, pl.ds(offset, part)]).astype(BF)


def attend_call(place, query, mine, other, wimg, wtxt):
    rows, part = query.shape

    def whole(shape):
        return pl.BlockSpec(shape, lambda i, s: (0,) * len(shape))

    return pl.pallas_call(
        attend_kernel,
        out_shape=jax.ShapeDtypeStruct((4, rows, part), BF),
        grid_spec=pltpu.PrefetchScalarGridSpec(
            num_scalar_prefetch=1,
            grid=(1,),
            in_specs=[whole(a.shape) for a in (query, mine, other, wimg, wtxt)],
            out_specs=whole((4, rows, part)),
            scratch_shapes=[pltpu.VMEM((rows, part), BF)],
        ),
        compiler_params=pltpu.CompilerParams(
            dimension_semantics=("arbitrary",), vmem_limit_bytes=VMEM_LIMIT
        ),
        cost_estimate=pl.CostEstimate(
            flops=4 * rows * rows * 2 * 6 * 256, transcendentals=rows * rows * 12, bytes_accessed=6 << 20
        ),
        name="attend",
    )(place, query, mine, other, wimg, wtxt)


def mlp_kernel(place_ref, x0, x1, x2, x3, imod_ref, up_ref, down_ref, out_ref, acts_ref, sum_ref):
    step = pl.program_id(0)
    blk = place_ref[0]
    part = x0.shape[1]

    @pl.when(step == 0)
    def _():
        pieces = [ref[...].astype(F32) for ref in (x0, x1, x2, x3)]
        mods = [imod_ref[blk ^ j] for j in range(4)]
        for j, value in enumerate(normed_acts(pieces, mods, 3, 4, 4 * part)):
            acts_ref[j] = value

    hidden = None
    for j in range(4):
        offset = pl.multiple_of((blk ^ j) * part, part)
        term = dot(acts_ref[j], up_ref[pl.ds(offset, part), :])
        hidden = term if hidden is None else hidden + term
    hidden = jax.nn.gelu(hidden, approximate=True).astype(BF)
    last = pl.num_programs(0) - 1
    for j in range(4):
        offset = pl.multiple_of((blk ^ j) * part, part)
        term = dot(hidden, down_ref[:, pl.ds(offset, part)])

        @pl.when(step == 0)
        def _():
            sum_ref[j] = term

        @pl.when((step > 0) & (step < last))
        def _():
            sum_ref[j] += term

        @pl.when(step == last)
        def _():
            out_ref[j] = (sum_ref[j] + term).astype(BF)


def mlp_call(place, pieces, imod, up, down):
    rows, part = pieces[0].shape
    width = 4 * part
    steps = 4
    span = up.shape[1] // steps

    def whole(shape):
        return pl.BlockSpec(shape, lambda i, s: (0,) * len(shape))

    return pl.pallas_call(
        mlp_kernel,
        out_shape=jax.ShapeDtypeStruct((4, rows, part), BF),
        grid_spec=pltpu.PrefetchScalarGridSpec(
            num_scalar_prefetch=1,
            grid=(steps,),
            in_specs=[whole((rows, part))] * 4
            + [
                whole(imod.shape),
                pl.BlockSpec((width, span), lambda i, s: (0, i)),
                pl.BlockSpec((span, width), lambda i, s: (i, 0)),
            ],
            out_specs=whole((4, rows, part)),
            scratch_shapes=[pltpu.VMEM((4, rows, part), BF), pltpu.VMEM((4, rows, part), F32)],
        ),
        compiler_params=pltpu.CompilerParams(
            dimension_semantics=("arbitrary",), vmem_limit_bytes=VMEM_LIMIT
        ),
        cost_estimate=pl.CostEstimate(
            flops=4 * rows * width * up.shape[1], transcendentals=rows * up.shape[1], bytes_accessed=12 << 20
        ),
        name="mlp",
    )(place, *pieces, imod, up, down)


def swap(values, axis, size, bit):
    return lax.ppermute(values, axis, [(i, i ^ bit) for i in range(size)])


def per_device(
    tiles,
    image_tokens,
    text_tokens,
    step_index,
    text_length,
    image_table,
    text_table,
    qkv_image,
    qkv_text,
    attn_out_image,
    attn_out_text,
    query_gain_image,
    key_gain_image,
    query_gain_text,
    key_gain_text,
    up_weight,
    down_weight,
):
    requests, image_rows, part = image_tokens.shape
    text_rows = text_tokens.shape[1]
    tile = lax.axis_index("tile")
    blk = lax.axis_index("blk")
    groups = [[t for t in range(tiles) if (t >> 2) & 1 == p] for p in (0, 1)]
    parity = (tile >> 2) & 1
    request = (tile >> 3) * 4 + (tile & 3)
    place = jnp.stack([blk, parity, text_length[request]]).astype(jnp.int32)

    step = step_index[request]
    imod = lax.dynamic_index_in_dim(image_table, step, 0, keepdims=False).astype(F32)
    tmod = lax.dynamic_index_in_dim(text_table, step, 0, keepdims=False).astype(F32)
    imod = jnp.transpose(imod.reshape(6, 4, part), (1, 0, 2))
    tmod = jnp.transpose(tmod.reshape(3, 4, part), (1, 0, 2))
    imod_own = lax.dynamic_index_in_dim(imod, blk, 0, keepdims=False)
    tmod_own = lax.dynamic_index_in_dim(tmod, blk, 0, keepdims=False)

    packed = jnp.concatenate(
        [image_tokens, jnp.pad(text_tokens, ((0, 0), (0, TXT_PAD - text_rows), (0, 0)))], axis=1
    )
    own = lax.all_to_all(packed, "tile", 0, 0, axis_index_groups=groups, tiled=True)
    far = swap(own, "blk", 4, 2)
    near = swap(own, "blk", 4, 1)
    diag = swap(far, "blk", 4, 1)

    wimg = jnp.transpose(qkv_image, (1, 0, 2))
    wtxt = jnp.transpose(qkv_text, (1, 0, 2))
    heads = part // HEAD_DIM
    gains = jnp.stack(
        [jnp.tile(g, heads) for g in (query_gain_image, query_gain_text, key_gain_image, key_gain_text)]
    )
    index = jnp.arange(part) // HEAD_DIM
    group = jnp.where(index[:, None] == index[None, :], 1.0 / HEAD_DIM, 0.0).astype(BF)

    query, mine = qkv_call(place, [own, near, far, diag], imod, tmod, wimg, wtxt, gains, group)
    other = swap(mine, "tile", tiles, 4)
    terms = attend_call(place, query, mine, other, attn_out_image, attn_out_text)

    def scatter(blocks):
        came = swap(jnp.stack([blocks[1], blocks[3]]), "blk", 4, 1)
        away = (blocks[2].astype(F32) + came[1].astype(F32)).astype(BF)
        back = swap(away, "blk", 4, 2)
        return blocks[0].astype(F32) + came[0].astype(F32) + back.astype(F32)

    proj = scatter(terms)
    img_rows = requests * image_rows
    image_own = own[:, :image_rows].reshape(img_rows, part)
    text_own = own[:, image_rows:].reshape(requests * TXT_PAD, part)
    image_mid = (image_own.astype(F32) + imod_own[2:3] * proj[:img_rows]).astype(BF)
    text_out = (text_own.astype(F32) + tmod_own[2:3] * proj[img_rows:]).astype(BF)
    mid_far = swap(image_mid, "blk", 4, 2)
    mid_near = swap(image_mid, "blk", 4, 1)
    mid_diag = swap(mid_far, "blk", 4, 1)
    downs = mlp_call(place, [image_mid, mid_near, mid_far, mid_diag], imod, up_weight, down_weight)
    image_out = (image_mid.astype(F32) + imod_own[5:6] * scatter(downs)).astype(BF)

    result = jnp.concatenate(
        [image_out.reshape(requests, image_rows, part), text_out.reshape(requests, TXT_PAD, part)], axis=1
    )
    result = lax.all_to_all(result, "tile", 0, 0, axis_index_groups=groups, tiled=True)
    return (result[:, :image_rows], result[:, image_rows : image_rows + text_rows])


def solution(mesh):
    in_specs = (
        P(None, "tile", "blk"),
        P(None, "tile", "blk"),
        P(),
        P(),
        P(),
        P(),
        P(None, None, "blk"),
        P(None, None, "blk"),
        P("blk", None),
        P("blk", None),
        P(),
        P(),
        P(),
        P(),
        P(None, "blk"),
        P("blk", None),
    )
    out_specs = (P(None, "tile", "blk"), P(None, "tile", "blk"))
    return jax.shard_map(
        functools.partial(per_device, mesh.shape["tile"]),
        mesh=mesh,
        in_specs=in_specs,
        out_specs=out_specs,
        check_vma=False,
    )
```

```python
import functools

import jax
import jax.numpy as jnp
from jax import lax
from jax.experimental import pallas as pl
from jax.experimental.pallas import tpu as pltpu
from jax.sharding import PartitionSpec as P

HEAD_DIM = 64
BF = jnp.bfloat16
F32 = jnp.float32
HIDDEN_BIAS = -32768.0
TXT_PAD = 8
VMEM_LIMIT = 24 << 20
VM = pl.BlockSpec(memory_space=pltpu.VMEM)
SM = pl.BlockSpec(memory_space=pltpu.SMEM)


def dot(left, right):
    return jnp.dot(left, right, preferred_element_type=F32)


def dot_t(left, right):
    return lax.dot_general(left, right, (((1,), (1,)), ((), ())), preferred_element_type=F32)


def my_request():
    tile = lax.axis_index("tile")
    return (tile >> 2) * 2 + (tile & 1)


def table_rows(table_ref, step, rows):
    plane = table_ref[rows[0]]
    here = lax.broadcasted_iota(jnp.int32, plane.shape, 0) == step
    return [
        jnp.sum(jnp.where(here, table_ref[row].astype(F32), 0.0), axis=0, keepdims=True) for row in rows
    ]


def norm_rows(raw_ref, acts_ref, start, count, shift, scale, block=32):
    width = raw_ref.shape[1]
    gain = 1.0 + scale

    def body(i, carry):
        rows = pl.ds(pl.multiple_of(start + i * block, block), block)
        values = raw_ref[rows, :].astype(F32)
        centre = jnp.sum(values, axis=-1, keepdims=True) * (1.0 / width)
        moved = values - centre
        spread = jnp.sum(moved * moved, axis=-1, keepdims=True) * (1.0 / width)
        acts_ref[rows, :] = (moved * lax.rsqrt(spread + 1e-06) * gain + shift).astype(BF)
        return carry

    lax.fori_loop(0, count // block, body, 0, unroll=2)


def head_scale(values, group):
    parts = []
    for col in range(0, values.shape[1], 128):
        piece = values[:, col : col + 128]
        squares = piece * piece
        high = squares.astype(BF)
        low = (squares - high.astype(F32)).astype(BF)
        parts.append(dot(jnp.concatenate([high, low], axis=1), group))
    return lax.rsqrt(jnp.concatenate(parts, axis=1) + 1e-06)


def group_matrix():
    row = lax.broadcasted_iota(jnp.int32, (256, 128), 0)
    col = lax.broadcasted_iota(jnp.int32, (256, 128), 1)
    same = ((row & 127) >> 6) == (col >> 6)
    return jnp.where(same, 1.0 / HEAD_DIM, 0.0).astype(BF)


def wide_gain(ref, width):
    pair = jnp.concatenate([ref[...], ref[...]], axis=1)
    return jnp.concatenate([pair] * (width // 128), axis=1)


def qkv_kernel(first, sources, with_query, *refs):
    step_ref, x0, x1, x2, x3, itab, ttab, wimg, wtxt, gqi, gki, gqt, gkt = refs[:13]
    outs, (raw_ref, acts_ref) = refs[13:-2], refs[-2:]
    blk = lax.axis_index("blk")
    step = step_ref[my_request()]
    part = x0.shape[2]
    image_rows = x0.shape[1] - TXT_PAD
    img, txt = sources * image_rows, sources * TXT_PAD
    for j, (ref, begin) in enumerate(zip((x0, x1, x2, x3), first)):
        cols = pl.ds(pl.multiple_of((blk ^ j) * part, part), part)
        raw_ref[:img, cols] = ref[begin : begin + sources, :image_rows, :].reshape(img, part)
        text = ref[begin : begin + sources, image_rows:, :].astype(F32).reshape(txt, part)
        raw_ref[img:, cols] = text.astype(BF)
    shift, scale = table_rows(itab, step, (0, 1))
    norm_rows(raw_ref, acts_ref, 0, img, shift, scale)
    shift, scale = table_rows(ttab, step, (0, 1))
    norm_rows(raw_ref, acts_ref, img, txt, shift, scale)
    group = group_matrix()
    kv_ref = outs[-1]
    for w_ref, begin, end, query_gain, key_gain in (
        (wtxt, img, img + txt, gqt, gkt),
        (wimg, 0, img, gqi, gki),
    ):
        acts = acts_ref[begin:end, :]
        values = dot(acts, w_ref[1])
        kv_ref[0, begin:end, :] = (values * head_scale(values, group) * wide_gain(key_gain, part)).astype(BF)
        kv_ref[1, begin:end, :] = dot(acts, w_ref[2]).astype(BF)
        if with_query:
            values = dot(acts, w_ref[0])
            normed = (values * head_scale(values, group) * wide_gain(query_gain, part)).astype(BF)
            outs[0][begin:end, :] = normed * BF(HEAD_DIM**-0.5)


def qkv_call(step_index, pieces, first, sources, tables, weights, gains, with_query):
    part = pieces[0].shape[2]
    rows = sources * pieces[0].shape[1]
    outs = [jax.ShapeDtypeStruct((2, rows, part), BF)]
    if with_query:
        outs = [jax.ShapeDtypeStruct((rows, part), BF)] + outs
    return pl.pallas_call(
        functools.partial(qkv_kernel, first, sources, with_query),
        out_shape=outs,
        in_specs=[SM] + [VM] * 12,
        out_specs=[VM] * len(outs),
        scratch_shapes=[pltpu.VMEM((rows, 4 * part), BF), pltpu.VMEM((rows, 4 * part), BF)],
        compiler_params=pltpu.CompilerParams(vmem_limit_bytes=VMEM_LIMIT),
        cost_estimate=pl.CostEstimate(
            flops=rows * 6000000, transcendentals=0, bytes_accessed=rows * 4096
        ),
        name="qkv",
    )(step_index, *pieces, *tables, *weights, *gains)


def key_bias(length, rows, img_rows, parity, source_start):
    inner = lax.broadcasted_iota(jnp.int32, (rows - img_rows, 128), 0)
    source = (inner >> 3) + source_start
    slot = inner & 7
    tile = (source >> 1) * 4 + parity * 2 + (source & 1)
    seen = (slot < 5) & (tile * 5 + slot < length)
    return jnp.concatenate(
        [jnp.zeros((img_rows, 128), F32), jnp.where(seen, 0.0, HIDDEN_BIAS)], axis=0
    ).astype(BF)


def store_blocks(value, pair, odd, keep_ref, send_ref):
    part = keep_ref.shape[2]
    low, high = value[:, :part].astype(BF), value[:, part:].astype(BF)

    @pl.when(odd == 0)
    def _():
        keep_ref[pair] = low
        send_ref[pair] = high

    @pl.when(odd == 1)
    def _():
        keep_ref[pair] = high
        send_ref[pair] = low


def attend_kernel(start, count, gate_row, *refs):
    step_ref, length_ref, q_ref, kv_ref, ka_ref, kb_ref, table, w_ref, keep_ref, send_ref = refs
    blk = lax.axis_index("blk")
    parity = (lax.axis_index("tile") >> 1) & 1
    request = my_request()
    step, length = step_ref[request], length_ref[request]
    part = q_ref.shape[1]
    lane = lax.broadcasted_iota(jnp.int32, (count, 128), 1)
    one_lane = jnp.where(lane == 0, 1.0, 0.0).astype(BF)
    key_refs = (kv_ref, ka_ref, kb_ref)
    biases = []
    for ref, side, source in zip(key_refs, (0, 1, 1), (0, 0, 8)):
        rows = ref.shape[1]
        biases.append(key_bias(length, rows, rows // 5 * 4, parity ^ side, source))
    att = []
    for col in range(0, part, 128):
        cols = slice(col, col + 128)
        keys = [jnp.concatenate([ref[0, :, cols], bias], axis=1) for ref, bias in zip(key_refs, biases)]
        vals = [
            jnp.concatenate([ref[1, :, cols], jnp.ones((ref.shape[1], 128), BF)], axis=1) for ref in key_refs
        ]
        query = q_ref[start : start + count, cols]
        outs = []
        for head in range(2):
            mine = (lane < 64) if head == 0 else (lane >= 64)
            left = jnp.concatenate([jnp.where(mine, query, BF(0.0)), one_lane], axis=1)
            scores = [dot_t(left, key) for key in keys]
            tops = [jnp.max(score, axis=-1, keepdims=True) for score in scores]
            top = functools.reduce(jnp.maximum, tops)
            both = sum(dot(jnp.exp(score - top).astype(BF), val) for score, val in zip(scores, vals))
            outs.append(both[:, :128] / both[:, 128:])
        att.append(jnp.where(lane < 64, outs[0], outs[1]).astype(BF))
    att = jnp.concatenate(att, axis=1)
    gate = table_rows(table, step, (gate_row,))[0]
    project_out(att, gate, w_ref, blk, keep_ref, send_ref)


def project_out(left, gate, w_ref, blk, keep_ref, send_ref):
    part = keep_ref.shape[2]
    for pair in range(2):
        which = (blk >> 1) ^ pair
        value = dot(left, w_ref[:, pl.ds(pl.multiple_of(which * 2 * part, 2 * part), 2 * part)])
        width = gate.shape[1]
        mine = jnp.where(which == 0, gate[:, : width // 2], gate[:, width // 2 :])
        store_blocks(value * mine, pair, blk & 1, keep_ref, send_ref)


def attend_call(step_index, lengths, query, keys, start, count, table, gate_row, weight):
    part = query.shape[1]
    shape = jax.ShapeDtypeStruct((2, count, part), BF)
    return pl.pallas_call(
        functools.partial(attend_kernel, start, count, gate_row),
        out_shape=[shape, shape],
        in_specs=[SM, SM] + [VM] * 6,
        out_specs=[VM, VM],
        compiler_params=pltpu.CompilerParams(vmem_limit_bytes=VMEM_LIMIT),
        cost_estimate=pl.CostEstimate(
            flops=count * 16000000, transcendentals=0, bytes_accessed=count * 4096
        ),
        name="attend",
    )(step_index, lengths, query, *keys, table, weight)


def mlp_kernel(step_ref, x0, x1, x2, x3, table, up_ref, down_ref, keep_ref, send_ref, raw_ref, acts_ref):
    blk = lax.axis_index("blk")
    step = step_ref[my_request()]
    rows, part = x0.shape
    for j, ref in enumerate((x0, x1, x2, x3)):
        raw_ref[:, pl.ds(pl.multiple_of((blk ^ j) * part, part), part)] = ref[...]
    shift, scale, gate = table_rows(table, step, (3, 4, 5))
    norm_rows(raw_ref, acts_ref, 0, rows, shift, scale)
    for col in range(0, up_ref.shape[1], 512):
        hidden = dot(acts_ref[...], up_ref[:, col : col + 512])
        raw_ref[:, col : col + 512] = jax.nn.gelu(hidden, approximate=True).astype(BF)
    project_out(raw_ref[...], gate, down_ref, blk, keep_ref, send_ref)


def mlp_call(step_index, pieces, table, up, down):
    rows, part = pieces[0].shape
    shape = jax.ShapeDtypeStruct((2, rows, part), BF)
    return pl.pallas_call(
        mlp_kernel,
        out_shape=[shape, shape],
        in_specs=[SM] + [VM] * 7,
        out_specs=[VM, VM],
        scratch_shapes=[pltpu.VMEM((rows, 4 * part), BF), pltpu.VMEM((rows, 4 * part), BF)],
        compiler_params=pltpu.CompilerParams(vmem_limit_bytes=VMEM_LIMIT),
        cost_estimate=pl.CostEstimate(
            flops=rows * 16000000, transcendentals=0, bytes_accessed=rows * 4096
        ),
        name="mlp",
    )(step_index, *pieces, table, up, down)


def swap(values, axis, size, bit):
    return lax.ppermute(values, axis, [(i, i ^ bit) for i in range(size)])


def add(*terms):
    return sum(term.astype(F32) for term in terms).astype(BF)


def per_device(
    tiles,
    image_tokens,
    text_tokens,
    step_index,
    text_length,
    image_table,
    text_table,
    qkv_image,
    qkv_text,
    attn_out_image,
    attn_out_text,
    query_gain_image,
    key_gain_image,
    query_gain_text,
    key_gain_text,
    up_weight,
    down_weight,
):
    requests, image_rows, part = image_tokens.shape
    text_rows = text_tokens.shape[1]
    half = requests // 2
    groups = [[t for t in range(tiles) if (t >> 1) & 1 == p] for p in (0, 1)]
    tables = [jnp.transpose(table, (1, 0, 2)) for table in (image_table, text_table)]
    weights = [jnp.transpose(weight, (1, 0, 2)) for weight in (qkv_image, qkv_text)]
    gains = [
        gain.reshape(1, HEAD_DIM)
        for gain in (query_gain_image, key_gain_image, query_gain_text, key_gain_text)
    ]

    packed = jnp.concatenate(
        [image_tokens, jnp.pad(text_tokens, ((0, 0), (0, TXT_PAD - text_rows), (0, 0)))], axis=1
    )
    own = lax.all_to_all(packed, "tile", 0, 0, axis_index_groups=groups, tiled=True)
    far = swap(own, "blk", 4, 2)
    other = swap(own, "tile", tiles, 2)
    near = swap(own, "blk", 4, 1)
    diag = swap(far, "blk", 4, 1)
    other_far = [swap(other[c * half : c * half + half], "blk", 4, 2) for c in range(2)]
    other_near = swap(other, "blk", 4, 1)

    query, mine = qkv_call(
        step_index, [own, near, far, diag], (0, 0, 0, 0), requests, tables, weights, gains, True
    )
    keys = [mine]
    for c in range(2):
        other_diag = swap(other_far[c], "blk", 4, 1)
        begin = c * half
        keys += qkv_call(
            step_index, [other, other_near, other_far[c], other_diag], (begin, begin, 0, 0), half,
            tables, weights, gains, False,
        )

    def attend(start, count, table, weight):
        return attend_call(step_index, text_length, query, keys, start, count, table, 2, weight)

    def scatter(keep, send):
        came = swap(send, "blk", 4, 1)
        back = swap(add(keep[1], came[1]), "blk", 4, 2)
        return keep[0], came[0], back

    img_rows = requests * image_rows
    chunk = img_rows // 2
    mids, downs = [], []
    shares = [attend(c * chunk, chunk, tables[0], attn_out_image) for c in range(2)]
    text_share = attend(img_rows, requests * TXT_PAD, tables[1], attn_out_text)
    for c in range(2):
        start = own[c * half : c * half + half, :image_rows].reshape(chunk, part)
        mids.append(add(start, *scatter(*shares[c])))
    text_own = own[:, image_rows:].reshape(requests * TXT_PAD, part)
    text_out = add(text_own, *scatter(*text_share))
    for mid in mids:
        mid_far = swap(mid, "blk", 4, 2)
        mid_near = swap(mid, "blk", 4, 1)
        mid_diag = swap(mid_far, "blk", 4, 1)
        downs.append(
            mlp_call(step_index, [mid, mid_near, mid_far, mid_diag], tables[0], up_weight, down_weight)
        )
    image_out = [add(mid, *scatter(*down)) for mid, down in zip(mids, downs)]

    result = jnp.concatenate(
        [
            jnp.concatenate(image_out, axis=0).reshape(requests, image_rows, part),
            text_out.reshape(requests, TXT_PAD, part),
        ],
        axis=1,
    )
    result = lax.all_to_all(result, "tile", 0, 0, axis_index_groups=groups, tiled=True)
    return (result[:, :image_rows], result[:, image_rows : image_rows + text_rows])


def solution(mesh):
    in_specs = (
        P(None, "tile", "blk"),
        P(None, "tile", "blk"),
        P(),
        P(),
        P(),
        P(),
        P(None, None, "blk"),
        P(None, None, "blk"),
        P("blk", None),
        P("blk", None),
        P(),
        P(),
        P(),
        P(),
        P(None, "blk"),
        P("blk", None),
    )
    out_specs = (P(None, "tile", "blk"), P(None, "tile", "blk"))
    return jax.shard_map(
        functools.partial(per_device, mesh.shape["tile"]),
        mesh=mesh,
        in_specs=in_specs,
        out_specs=out_specs,
        check_vma=False,
    )
```

```python
import functools

import jax
import jax.numpy as jnp
from jax import lax
from jax.experimental import pallas as pl
from jax.experimental.pallas import tpu as pltpu
from jax.sharding import PartitionSpec as P

HEAD_DIM = 64
BF = jnp.bfloat16
F32 = jnp.float32
HIDDEN_BIAS = -32768.0
TXT_PAD = 8
VMEM_LIMIT = 28 << 20
VM = pl.BlockSpec(memory_space=pltpu.VMEM)
SM = pl.BlockSpec(memory_space=pltpu.SMEM)
HB = pl.BlockSpec(memory_space=pltpu.HBM)
COST = pl.CostEstimate(flops=1, transcendentals=0, bytes_accessed=1)


def dot(left, right):
    return jnp.dot(left, right, preferred_element_type=F32)


def dot_t(left, right):
    return lax.dot_general(left, right, (((1,), (1,)), ((), ())), preferred_element_type=F32)


def pinned(*arrays):
    return [pltpu.with_memory_space_constraint(array, pltpu.HBM) for array in arrays]


def fetch(sources, targets, sems):
    copies = [
        pltpu.make_async_copy(source, target, sems.at[i])
        for i, (source, target) in enumerate(zip(sources, targets))
    ]
    for copy in copies:
        copy.start()
    return copies


def table_row(table_ref, step, row):
    plane = table_ref[row].astype(F32)
    here = lax.broadcasted_iota(jnp.int32, plane.shape, 0) == step
    return jnp.sum(jnp.where(here, plane, 0.0), axis=0, keepdims=True)


def prep_kernel(step_ref, length_ref, *refs):
    mods_ref, gains_ref, bias_ref = refs[6:9]
    copies = fetch(refs[:6], refs[9:15], refs[15])
    for copy in copies:
        copy.wait()
    itab, ttab, gqi, gki, gqt, gkt = refs[9:15]
    tile = lax.axis_index("tile")
    request = (tile >> 2) * 2 + (tile & 1)
    step, length = step_ref[request], length_ref[request]
    for row in range(6):
        mods_ref[row : row + 1, :] = table_row(itab, step, row)
    for row in range(3):
        mods_ref[8 + row : 9 + row, :] = table_row(ttab, step, row)
    for row, ref in enumerate((gqi, gki, gqt, gkt)):
        gains_ref[row : row + 1, :] = jnp.concatenate([ref[...], ref[...]], axis=1)
    inner = lax.broadcasted_iota(jnp.int32, bias_ref.shape[1:], 0)
    source, slot = inner >> 3, inner & 7
    for side in range(2):
        parity = ((tile >> 1) & 1) ^ side
        sender = (source >> 1) * 4 + parity * 2 + (source & 1)
        seen = (slot < 5) & (sender * 5 + slot < length)
        bias_ref[side] = jnp.where(seen, 0.0, HIDDEN_BIAS).astype(BF)


def prep_call(step_index, text_length, tables, gains):
    width = tables[0].shape[2]
    return pl.pallas_call(
        prep_kernel,
        out_shape=[
            jax.ShapeDtypeStruct((16, width), F32),
            jax.ShapeDtypeStruct((8, 128), F32),
            jax.ShapeDtypeStruct((2, 128, 128), BF),
        ],
        in_specs=[SM, SM] + [HB] * 6,
        out_specs=[VM] * 3,
        scratch_shapes=[pltpu.VMEM(x.shape, x.dtype) for x in (*tables, *gains)]
        + [pltpu.SemaphoreType.DMA((6,))],
        compiler_params=pltpu.CompilerParams(vmem_limit_bytes=VMEM_LIMIT),
        cost_estimate=COST,
        name="prep",
    )(step_index, text_length, *pinned(*tables, *gains))


def norm_rows(raw_ref, acts_ref, start, count, shift, scale, block=32):
    width = raw_ref.shape[1]
    gain = 1.0 + scale

    def body(i, carry):
        rows = pl.ds(pl.multiple_of(start + i * block, block), block)
        values = raw_ref[rows, :].astype(F32)
        centre = jnp.sum(values, axis=-1, keepdims=True) * (1.0 / width)
        moved = values - centre
        spread = jnp.sum(moved * moved, axis=-1, keepdims=True) * (1.0 / width)
        acts_ref[rows, :] = (moved * lax.rsqrt(spread + 1e-06) * gain + shift).astype(BF)
        return carry

    lax.fori_loop(0, count // block, body, 0, unroll=2)


def head_scale(values, group):
    parts = []
    for col in range(0, values.shape[1], 128):
        piece = values[:, col : col + 128]
        squares = piece * piece
        high = squares.astype(BF)
        low = (squares - high.astype(F32)).astype(BF)
        parts.append(dot(jnp.concatenate([high, low], axis=1), group))
    return lax.rsqrt(jnp.concatenate(parts, axis=1) + 1e-06)


def group_matrix():
    row = lax.broadcasted_iota(jnp.int32, (256, 128), 0)
    col = lax.broadcasted_iota(jnp.int32, (256, 128), 1)
    same = ((row & 127) >> 6) == (col >> 6)
    return jnp.where(same, 1.0 / HEAD_DIM, 0.0).astype(BF)


def qkv_kernel(begin, sources, parts, *refs):
    mods, gains, x0, x1, x2, x3, wimg, wtxt = refs[:8]
    outs, (wimg_ref, wtxt_ref, raw_ref, acts_ref, sems) = refs[8:-5], refs[-5:]
    copies = fetch(
        [w.at[i] for w in (wtxt, wimg) for i in parts],
        [
            w.at[:, i * x0.shape[2] : (i + 1) * x0.shape[2]]
            for w in (wtxt_ref, wimg_ref)
            for i in range(len(parts))
        ],
        sems,
    )
    blk = lax.axis_index("blk")
    part = x0.shape[2]
    image_rows = x0.shape[1] - TXT_PAD
    img, txt = sources * image_rows, sources * TXT_PAD
    for j, (ref, first) in enumerate(zip((x0, x1, x2, x3), begin)):
        cols = pl.ds(pl.multiple_of((blk ^ j) * part, part), part)
        raw_ref[:img, cols] = ref[first : first + sources, :image_rows, :].reshape(img, part)
        text = ref[first : first + sources, image_rows:, :].astype(F32).reshape(txt, part)
        raw_ref[img:, cols] = text.astype(BF)
    norm_rows(raw_ref, acts_ref, img, txt, mods[8:9, :], mods[9:10, :])
    norm_rows(raw_ref, acts_ref, 0, img, mods[0:1, :], mods[1:2, :])
    group = group_matrix()
    kv_ref = outs[-1]
    for w_ref, first, last, row, waits in (
        (wtxt_ref, img, img + txt, 2, copies[: len(parts)]),
        (wimg_ref, 0, img, 0, copies[len(parts) :]),
    ):
        for copy in waits:
            copy.wait()
        projected = dot(acts_ref[first:last, :], w_ref[...])
        for i, which in enumerate(parts):
            values = projected[:, i * part : (i + 1) * part]
            if which == 2:
                kv_ref[1, first:last, :] = values.astype(BF)
                continue
            gain = jnp.concatenate([gains[row + which : row + which + 1, :]] * (part // 128), axis=1)
            normed = (values * head_scale(values, group) * gain).astype(BF)
            if which == 1:
                kv_ref[0, first:last, :] = normed
            else:
                outs[0][first:last, :] = normed * BF(HEAD_DIM**-0.5)


def qkv_call(mods, gains, pieces, begin, sources, weights, parts):
    part = pieces[0].shape[2]
    rows, width = sources * pieces[0].shape[1], 4 * part
    outs = [jax.ShapeDtypeStruct((2, rows, part), BF)]
    if 0 in parts:
        outs = [jax.ShapeDtypeStruct((rows, part), BF)] + outs
    weight = pltpu.VMEM((width, len(parts) * part), BF)
    return pl.pallas_call(
        functools.partial(qkv_kernel, begin, sources, parts),
        out_shape=outs,
        in_specs=[VM] * 6 + [HB] * 2,
        out_specs=[VM] * len(outs),
        scratch_shapes=[weight, weight]
        + [pltpu.VMEM((rows, width), BF)] * 2
        + [pltpu.SemaphoreType.DMA((2 * len(parts),))],
        compiler_params=pltpu.CompilerParams(vmem_limit_bytes=VMEM_LIMIT),
        cost_estimate=COST,
        name="qkv",
    )(mods, gains, *pieces, *pinned(*weights))


def head_scores(query, keys, lane, one_lane, head):
    mine = (lane < 64) if head == 0 else (lane >= 64)
    left = jnp.concatenate([jnp.where(mine, query, BF(0.0)), one_lane], axis=1)
    return [dot_t(left, key) for key in keys]


def both_halves(values, lane):
    return jnp.where(lane < 64, values[0], values[1])


def lane_masks(rows):
    lane = lax.broadcasted_iota(jnp.int32, (rows, 128), 1)
    return lane, jnp.where(lane == 0, 1.0, 0.0).astype(BF)


def hiding(bias, img_rows):
    return jnp.concatenate([jnp.zeros((img_rows, 128), BF), bias], axis=0)


def biased(ref, bias, cols):
    return jnp.concatenate([ref[0, :, cols], bias], axis=1)


def summed(ref, cols):
    return jnp.concatenate([ref[1, :, cols], jnp.ones((ref.shape[1], 128), BF)], axis=1)


def own_kernel(bias_ref, q_ref, kv_ref, top_ref, sum_ref, out_ref):
    rows, part = q_ref.shape
    count = rows // 2
    bias = hiding(bias_ref[0], rows - bias_ref.shape[1])
    lane, one_lane = lane_masks(count)
    for col in range(0, part, 128):
        cols = slice(col, col + 128)
        key, value = biased(kv_ref, bias, cols), summed(kv_ref, cols)
        for start in range(0, rows, count):
            span = slice(start, start + count)
            tops, sums, outs = [], [], []
            for head in range(2):
                score = head_scores(q_ref[span, cols], [key], lane, one_lane, head)[0]
                top = jnp.max(score, axis=-1, keepdims=True)
                both = dot(jnp.exp(score - top).astype(BF), value)
                tops.append(top)
                outs.append(both[:, :128])
                sums.append(both[:, 128:])
            top_ref[span, cols] = both_halves(tops, lane)
            sum_ref[span, cols] = both_halves(sums, lane)
            out_ref[span, cols] = both_halves(outs, lane)


def own_call(bias, query, keys):
    shape = jax.ShapeDtypeStruct(query.shape, F32)
    return pl.pallas_call(
        own_kernel,
        out_shape=[shape] * 3,
        in_specs=[VM] * 3,
        out_specs=[VM] * 3,
        compiler_params=pltpu.CompilerParams(vmem_limit_bytes=VMEM_LIMIT),
        cost_estimate=COST,
        name="attend_own",
    )(bias, query, keys)


def attend_kernel(start, counts, gate_rows, *refs):
    groups = len(counts)
    count = sum(counts)
    mods, bias_ref, q_ref, top_ref, sum_ref, out_ref, kv_ref = refs[:7]
    w_refs, sems = refs[7 + 3 * groups : -1], refs[-1]
    copies = fetch(refs[7 : 7 + groups], w_refs, sems)
    part = q_ref.shape[1]
    lane, one_lane = lane_masks(count)
    bias = hiding(bias_ref[1], kv_ref.shape[1] - bias_ref.shape[1])
    span = slice(start, start + count)
    att = []
    for col in range(0, part, 128):
        cols = slice(col, col + 128)
        key, val = biased(kv_ref, bias, cols), summed(kv_ref, cols)
        outs, sums, scales = [], [], []
        for head in range(2):
            score = head_scores(q_ref[span, cols], [key], lane, one_lane, head)[0]
            before = top_ref[span, col + 64 * head : col + 64 * head + 1]
            top = jnp.maximum(before, jnp.max(score, axis=-1, keepdims=True))
            both = dot(jnp.exp(score - top).astype(BF), val)
            outs.append(both[:, :128])
            sums.append(both[:, 128:])
            scales.append(jnp.exp(before - top))
        scale = both_halves(scales, lane)
        total = both_halves(sums, lane) + scale * sum_ref[span, cols]
        att.append(((both_halves(outs, lane) + scale * out_ref[span, cols]) / total).astype(BF))
    att = jnp.concatenate(att, axis=1)
    first = 0
    for i, (rows, row) in enumerate(zip(counts, gate_rows)):
        copies[i].wait()
        outs = refs[7 + groups + 2 * i : 9 + groups + 2 * i]
        project_out(att[first : first + rows], mods[row : row + 1, :], w_refs[i], *outs)
        first += rows


def project_out(left, gate, w_ref, keep_ref, send_ref):
    blk = lax.axis_index("blk")
    part = keep_ref.shape[2]
    width = gate.shape[1]
    for pair in range(2):
        which = (blk >> 1) ^ pair
        value = dot(left, w_ref[:, pl.ds(pl.multiple_of(which * 2 * part, 2 * part), 2 * part)])
        value = value * jnp.where(which == 0, gate[:, : width // 2], gate[:, width // 2 :])
        low, high = value[:, :part].astype(BF), value[:, part:].astype(BF)

        @pl.when((blk & 1) == 0)
        def _():
            keep_ref[pair] = low
            send_ref[pair] = high

        @pl.when((blk & 1) == 1)
        def _():
            keep_ref[pair] = high
            send_ref[pair] = low


def attend_call(mods, bias, query, state, keys, start, counts, gate_rows, weights):
    shapes = []
    for count in counts:
        shapes += [jax.ShapeDtypeStruct((2, count, query.shape[1]), BF)] * 2
    return pl.pallas_call(
        functools.partial(attend_kernel, start, counts, gate_rows),
        out_shape=shapes,
        in_specs=[VM] * 7 + [HB] * len(weights),
        out_specs=[VM] * len(shapes),
        scratch_shapes=[pltpu.VMEM(weight.shape, BF) for weight in weights]
        + [pltpu.SemaphoreType.DMA((len(weights),))],
        compiler_params=pltpu.CompilerParams(vmem_limit_bytes=VMEM_LIMIT),
        cost_estimate=COST,
        name="attend",
    )(mods, bias, query, *state, keys, *pinned(*weights))


def mlp_kernel(mods, mine, near, up_ref, down_ref, keep_ref, send_ref, raw_ref, acts_ref):
    blk = lax.axis_index("blk")
    rows, part = mine.shape[1:]
    span = up_ref.shape[1] // 3
    for j in range(4):
        value = (near if j & 1 else mine)[j >> 1]
        raw_ref[:, pl.ds(pl.multiple_of((blk ^ j) * part, part), part)] = value
    norm_rows(raw_ref, acts_ref, 0, rows, mods[3:4, :], mods[4:5, :])
    for i in range(3):
        cols = slice(i * span, i * span + span)
        hidden = dot(acts_ref[...], up_ref[:, cols])
        raw_ref[:, cols] = jax.nn.gelu(hidden, approximate=True).astype(BF)
    project_out(raw_ref[...], mods[5:6, :], down_ref, keep_ref, send_ref)


def mlp_call(mods, mine, near, up, down):
    rows, part = mine.shape[1:]
    shape = jax.ShapeDtypeStruct((2, rows, part), BF)
    return pl.pallas_call(
        mlp_kernel,
        out_shape=[shape, shape],
        in_specs=[VM] * 5,
        out_specs=[VM, VM],
        scratch_shapes=[pltpu.VMEM((rows, 4 * part), BF)] * 2,
        compiler_params=pltpu.CompilerParams(vmem_limit_bytes=VMEM_LIMIT),
        cost_estimate=COST,
        name="mlp",
    )(mods, mine, near, up, down)


def swap(values, axis, size, bit):
    return lax.ppermute(values, axis, [(i, i ^ bit) for i in range(size)])


def after(value, *others):
    return lax.optimization_barrier((value, *others))[0]


def add(*terms):
    return sum(term.astype(F32) for term in terms).astype(BF)


def small_call(kernel, name, outs, args, scratch=(), spec=VM):
    return pl.pallas_call(
        kernel,
        out_shape=[jax.ShapeDtypeStruct(shape, BF) for shape in outs],
        in_specs=[spec] * len(args),
        out_specs=[VM] * len(outs),
        scratch_shapes=list(scratch),
        compiler_params=pltpu.CompilerParams(vmem_limit_bytes=VMEM_LIMIT),
        cost_estimate=COST,
        name=name,
    )(*args)


def pack_kernel(image, text, out_ref, slots_ref, text_ref, sems):
    requests, image_rows, part = image.shape
    copies = fetch((text, image), (text_ref, out_ref.at[:, :image_rows, :]), sems)
    copies[0].wait()
    slots_ref[...] = jnp.zeros_like(slots_ref)
    for slot in range(text_ref.shape[0]):
        value = text_ref[slot].astype(F32)
        for i in range(part // 128):
            slots_ref[i, pl.ds(slot, requests, stride=TXT_PAD), :] = value[:, i * 128 : i * 128 + 128]
    for i in range(part // 128):
        piece = slots_ref[i].reshape(requests, TXT_PAD, 128).astype(BF)
        out_ref[:, image_rows:, i * 128 : i * 128 + 128] = piece
    copies[1].wait()


def sum_kernel(first, left_ref, right_ref, out_ref):
    for i in range(first, 2):
        out_ref[i - first] = add(left_ref[i], right_ref[i])


def away_kernel(image_ref, came_i, text_ref, came_t, out_ref):
    rows = image_ref.shape[1]
    out_ref[:rows, :] = add(image_ref[1], came_i[1])
    out_ref[rows:, :] = add(text_ref[1], came_t[1])


def core_sum(kept, came, first):
    shape = (2 - first,) + kept.shape[1:]
    return small_call(functools.partial(sum_kernel, first), "core_sum", [shape], [kept, came])[0]


def middle_kernel(begin, own_ref, far_ref, sum_ref, back_ref, out_ref):
    rows, part = out_ref.shape[1:]
    image_rows = own_ref.shape[1] - TXT_PAD
    for i, ref in enumerate((own_ref, far_ref)):
        start = ref[begin : begin + rows // image_rows, :image_rows, :].reshape(rows, part)
        out_ref[i] = add(start, sum_ref[i], back_ref[1 - i])


def first_kernel(own_ref, keep_t, came_t, mid_a, keep_a, came_a, last_a, image_ref, text_ref):
    rows = image_ref.shape[0]
    image_ref[...] = add(mid_a[0], keep_a[0], came_a[0], last_a[:rows, :])
    sources, slots, part = own_ref.shape
    total = keep_t[0].astype(F32) + came_t[0].astype(F32) + last_a[rows:, :].astype(F32)
    text = own_ref[:, slots - TXT_PAD :, :].astype(F32) + total.reshape(sources, TXT_PAD, part)
    text_ref[...] = text.astype(BF)


def final_kernel(image_ref, text_ref, mid_b, keep_b, came_b, last_b, out_ref):
    sources, slots, part = out_ref.shape
    image_rows = slots - TXT_PAD
    half = sources // 2
    out_ref[:half, :image_rows, :] = image_ref[...].reshape(half, image_rows, part)
    value = add(mid_b[0], keep_b[0], came_b[0], last_b[0])
    out_ref[half:, :image_rows, :] = value.reshape(half, image_rows, part)
    out_ref[:, image_rows:, :] = text_ref[...]


def per_device(
    tiles,
    image_tokens,
    text_tokens,
    step_index,
    text_length,
    image_table,
    text_table,
    qkv_image,
    qkv_text,
    attn_out_image,
    attn_out_text,
    query_gain_image,
    key_gain_image,
    query_gain_text,
    key_gain_text,
    up_weight,
    down_weight,
):
    requests, image_rows, part = image_tokens.shape
    text_rows = text_tokens.shape[1]
    groups = [[t for t in range(tiles) if (t >> 1) & 1 == p] for p in (0, 1)]
    tables = [jnp.transpose(table, (1, 0, 2)) for table in (image_table, text_table)]
    weights = [jnp.transpose(weight, (1, 0, 2)) for weight in (qkv_image, qkv_text)]
    gains = [
        gain.reshape(1, HEAD_DIM)
        for gain in (query_gain_image, key_gain_image, query_gain_text, key_gain_text)
    ]

    slots = (requests, image_rows + TXT_PAD, part)
    text_slots = jnp.transpose(text_tokens, (1, 0, 2))
    packed = small_call(
        pack_kernel,
        "pack",
        [slots],
        pinned(image_tokens, text_slots),
        [
            pltpu.VMEM((part // 128, requests * TXT_PAD, 128), F32),
            pltpu.VMEM(text_slots.shape, BF),
            pltpu.SemaphoreType.DMA((2,)),
        ],
        HB,
    )[0]
    own = lax.all_to_all(packed, "tile", 0, 0, axis_index_groups=groups, tiled=True)
    far = swap(own, "blk", 4, 2)
    other = swap(own, "tile", tiles, 2)
    near = swap(own, "blk", 4, 1)
    mods, head_gains, bias = prep_call(after(step_index, own), text_length, tables, gains)

    def tied(*others):
        return after(mods, *others)

    def project(mods, pieces, parts):
        return qkv_call(mods, head_gains, pieces, (0, 0, 0, 0), requests, weights, parts)

    far = after(far, mods)
    other = after(other, far)
    other_far = swap(other, "blk", 4, 2)
    diag = swap(far, "blk", 4, 1)
    query, mine = project(mods, [own, near, far, diag], (1, 2, 0))
    other_near = swap(after(other, query), "blk", 4, 1)
    state = own_call(bias, query, mine)
    other_far = after(other_far, state[0])
    other_diag = swap(other_far, "blk", 4, 1)
    keys = project(tied(state[0]), [other, other_near, other_far, other_diag], (1, 2))[0]

    half = requests // 2
    rows = half * image_rows
    txt_rows = requests * TXT_PAD

    def attend(mods, *groups):
        return attend_call(mods, bias, query, state, keys, *groups)

    def middle(begin, sums, back):
        args = [own, far, sums, back]
        return small_call(functools.partial(middle_kernel, begin), "middle", [(2, rows, part)], args)[0]

    keep_a, send_a = attend(mods, 0, (rows,), (2,), (attn_out_image,))
    came_a = swap(send_a, "blk", 4, 1)
    sum_a = core_sum(keep_a, came_a, 0)
    back_a = swap(sum_a, "blk", 4, 2)
    keep_b, send_b, keep_t, send_t = attend(
        tied(sum_a), rows, (rows, txt_rows), (2, 10), (attn_out_image, attn_out_text)
    )
    came_b = swap(send_b, "blk", 4, 1)
    mid_a = middle(0, sum_a, after(back_a, keep_b))
    near_a = swap(mid_a, "blk", 4, 1)
    sum_b = core_sum(after(keep_b, mid_a), came_b, 0)
    back_b = swap(sum_b, "blk", 4, 2)
    came_t = swap(send_t, "blk", 4, 1)
    came_t = after(came_t, sum_b)
    down_a, send_a = mlp_call(tied(came_t), mid_a, near_a, up_weight, down_weight)
    came_a = swap(send_a, "blk", 4, 1)
    mid_b = middle(half, sum_b, after(back_b, down_a))
    near_b = swap(mid_b, "blk", 4, 1)
    args = [after(down_a, mid_b), came_a, keep_t, came_t]
    away_a = small_call(away_kernel, "away", [(rows + txt_rows, part)], args)[0]
    last_a = swap(away_a, "blk", 4, 2)
    down_b, send_b = mlp_call(tied(away_a), mid_b, near_b, up_weight, down_weight)
    args = [own, keep_t, came_t, mid_a, down_a, came_a, after(last_a, down_b)]
    image_a, text_out = small_call(
        first_kernel, "first", [(rows, part), (requests, TXT_PAD, part)], args
    )
    came_b = swap(after(send_b, image_a), "blk", 4, 1)
    away_b = core_sum(down_b, came_b, 1)
    last_b = swap(away_b, "blk", 4, 2)

    args = [image_a, text_out, mid_b, down_b, came_b, last_b]
    result = small_call(final_kernel, "final", [slots], args)[0]
    result = lax.all_to_all(result, "tile", 0, 0, axis_index_groups=groups, tiled=True)
    return (result[:, :image_rows], result[:, image_rows : image_rows + text_rows])


def solution(mesh):
    in_specs = (
        P(None, "tile", "blk"),
        P(None, "tile", "blk"),
        P(),
        P(),
        P(),
        P(),
        P(None, None, "blk"),
        P(None, None, "blk"),
        P("blk", None),
        P("blk", None),
        P(),
        P(),
        P(),
        P(),
        P(None, "blk"),
        P("blk", None),
    )
    out_specs = (P(None, "tile", "blk"), P(None, "tile", "blk"))
    return jax.shard_map(
        functools.partial(per_device, mesh.shape["tile"]),
        mesh=mesh,
        in_specs=in_specs,
        out_specs=out_specs,
        check_vma=False,
    )
```

```python
import functools

import jax
import jax.numpy as jnp
from jax import lax
from jax.experimental import pallas as pl
from jax.experimental.pallas import tpu as pltpu
from jax.sharding import PartitionSpec as P

HEAD_DIM = 64
BF = jnp.bfloat16
F32 = jnp.float32
HIDDEN_BIAS = -32768.0
TXT_PAD = 8
PARTS = (1, 2, 0)
VMEM_LIMIT = 28 << 20
VM = pl.BlockSpec(memory_space=pltpu.VMEM)
SM = pl.BlockSpec(memory_space=pltpu.SMEM)
HB = pl.BlockSpec(memory_space=pltpu.HBM)
COST = pl.CostEstimate(flops=1, transcendentals=0, bytes_accessed=1)


def dot(left, right):
    return jnp.dot(left, right, preferred_element_type=F32)


def dot_t(left, right):
    return lax.dot_general(left, right, (((1,), (1,)), ((), ())), preferred_element_type=F32)


def pinned(*arrays):
    return [pltpu.with_memory_space_constraint(array, pltpu.HBM) for array in arrays]


def fetch(sources, targets, sems):
    copies = [
        pltpu.make_async_copy(source, target, sems.at[i])
        for i, (source, target) in enumerate(zip(sources, targets))
    ]
    for copy in copies:
        copy.start()
    return copies


def table_row(table_ref, step, row):
    plane = table_ref[row].astype(F32)
    here = lax.broadcasted_iota(jnp.int32, plane.shape, 0) == step
    return jnp.sum(jnp.where(here, plane, 0.0), axis=0, keepdims=True)


def prep_kernel(step_ref, length_ref, *refs):
    mods_ref, gains_ref, bias_ref, wimg_ref, wtxt_ref = refs[8:13]
    part = refs[6].shape[2]
    sources, targets = list(refs[:6]), list(refs[13:19])
    for w, w_ref in zip(refs[6:8], (wimg_ref, wtxt_ref)):
        for i, which in enumerate(PARTS):
            sources.append(w.at[which])
            targets.append(w_ref.at[:, i * part : (i + 1) * part])
    copies = fetch(sources, targets, refs[19])
    for copy in copies[:6]:
        copy.wait()
    itab, ttab, gqi, gki, gqt, gkt = refs[13:19]
    tile = lax.axis_index("tile")
    request = (tile >> 2) * 2 + (tile & 1)
    step, length = step_ref[request], length_ref[request]
    for row in range(6):
        mods_ref[row : row + 1, :] = table_row(itab, step, row)
    for row in range(3):
        mods_ref[8 + row : 9 + row, :] = table_row(ttab, step, row)
    for row, ref in enumerate((gqi, gki, gqt, gkt)):
        gains_ref[row : row + 1, :] = jnp.concatenate([ref[...], ref[...]], axis=1)
    inner = lax.broadcasted_iota(jnp.int32, bias_ref.shape[1:], 0)
    source, slot = inner >> 3, inner & 7
    for side in range(2):
        parity = ((tile >> 1) & 1) ^ side
        sender = (source >> 1) * 4 + parity * 2 + (source & 1)
        seen = (slot < 5) & (sender * 5 + slot < length)
        bias_ref[side] = jnp.where(seen, 0.0, HIDDEN_BIAS).astype(BF)
    for copy in copies[6:]:
        copy.wait()


def prep_call(step_index, text_length, tables, gains, weights):
    width = tables[0].shape[2]
    wide = jax.ShapeDtypeStruct((width, 3 * weights[0].shape[2]), BF)
    return pl.pallas_call(
        prep_kernel,
        out_shape=[
            jax.ShapeDtypeStruct((16, width), F32),
            jax.ShapeDtypeStruct((8, 128), F32),
            jax.ShapeDtypeStruct((2, 128, 128), BF),
            wide,
            wide,
        ],
        in_specs=[SM, SM] + [HB] * 8,
        out_specs=[VM] * 5,
        scratch_shapes=[pltpu.VMEM(x.shape, x.dtype) for x in (*tables, *gains)]
        + [pltpu.SemaphoreType.DMA((12,))],
        compiler_params=pltpu.CompilerParams(vmem_limit_bytes=VMEM_LIMIT),
        cost_estimate=COST,
        name="prep",
    )(step_index, text_length, *pinned(*tables, *gains, *weights))


def norm_rows(raw_ref, acts_ref, start, count, shift, scale, block=32):
    width = raw_ref.shape[1]
    gain = 1.0 + scale

    def body(i, carry):
        rows = pl.ds(pl.multiple_of(start + i * block, block), block)
        values = raw_ref[rows, :].astype(F32)
        centre = jnp.sum(values, axis=-1, keepdims=True) * (1.0 / width)
        moved = values - centre
        spread = jnp.sum(moved * moved, axis=-1, keepdims=True) * (1.0 / width)
        acts_ref[rows, :] = (moved * lax.rsqrt(spread + 1e-06) * gain + shift).astype(BF)
        return carry

    lax.fori_loop(0, count // block, body, 0, unroll=4)


def head_scale(values, group):
    parts = []
    for col in range(0, values.shape[1], 128):
        piece = values[:, col : col + 128]
        squares = piece * piece
        high = squares.astype(BF)
        low = (squares - high.astype(F32)).astype(BF)
        parts.append(dot(jnp.concatenate([high, low], axis=1), group))
    return lax.rsqrt(jnp.concatenate(parts, axis=1) + 1e-06)


def group_matrix():
    row = lax.broadcasted_iota(jnp.int32, (256, 128), 0)
    col = lax.broadcasted_iota(jnp.int32, (256, 128), 1)
    same = ((row & 127) >> 6) == (col >> 6)
    return jnp.where(same, 1.0 / HEAD_DIM, 0.0).astype(BF)


def qkv_kernel(begin, sources, parts, *refs):
    mods, gains, x0, x1, x2, x3, wimg_ref, wtxt_ref = refs[:8]
    outs, (raw_ref, acts_ref) = refs[8:-2], refs[-2:]
    blk = lax.axis_index("blk")
    part = x0.shape[2]
    image_rows = x0.shape[1] - TXT_PAD
    img, txt = sources * image_rows, sources * TXT_PAD
    for j, (ref, first) in enumerate(zip((x0, x1, x2, x3), begin)):
        cols = pl.ds(pl.multiple_of((blk ^ j) * part, part), part)
        raw_ref[:img, cols] = ref[first : first + sources, :image_rows, :].reshape(img, part)
        text = ref[first : first + sources, image_rows:, :].astype(F32).reshape(txt, part)
        raw_ref[img:, cols] = text.astype(BF)
    norm_rows(raw_ref, acts_ref, img, txt, mods[8:9, :], mods[9:10, :])
    norm_rows(raw_ref, acts_ref, 0, img, mods[0:1, :], mods[1:2, :])
    group = group_matrix()
    kv_ref = outs[-1]
    for w_ref, first, last, row in ((wtxt_ref, img, img + txt, 2), (wimg_ref, 0, img, 0)):
        projected = dot(acts_ref[first:last, :], w_ref[:, : len(parts) * part])
        for i, which in enumerate(parts):
            values = projected[:, i * part : (i + 1) * part]
            if which == 2:
                kv_ref[1, first:last, :] = values.astype(BF)
                continue
            gain = jnp.concatenate([gains[row + which : row + which + 1, :]] * (part // 128), axis=1)
            normed = (values * head_scale(values, group) * gain).astype(BF)
            if which == 1:
                kv_ref[0, first:last, :] = normed
            else:
                outs[0][first:last, :] = normed * BF(HEAD_DIM**-0.5)


def qkv_call(mods, gains, pieces, begin, sources, weights, parts):
    part = pieces[0].shape[2]
    rows, width = sources * pieces[0].shape[1], 4 * part
    outs = [jax.ShapeDtypeStruct((2, rows, part), BF)]
    if 0 in parts:
        outs = [jax.ShapeDtypeStruct((rows, part), BF)] + outs
    return pl.pallas_call(
        functools.partial(qkv_kernel, begin, sources, parts),
        out_shape=outs,
        in_specs=[VM] * 8,
        out_specs=[VM] * len(outs),
        scratch_shapes=[pltpu.VMEM((rows, width), BF)] * 2,
        compiler_params=pltpu.CompilerParams(vmem_limit_bytes=VMEM_LIMIT),
        cost_estimate=COST,
        name="qkv",
    )(mods, gains, *pieces, *weights)


def head_scores(query, keys, lane, one_lane, head):
    mine = (lane < 64) if head == 0 else (lane >= 64)
    left = jnp.concatenate([jnp.where(mine, query, BF(0.0)), one_lane], axis=1)
    return [dot_t(left, key) for key in keys]


def both_halves(values, lane):
    return jnp.where(lane < 64, values[0], values[1])


def lane_masks(rows):
    lane = lax.broadcasted_iota(jnp.int32, (rows, 128), 1)
    return lane, jnp.where(lane == 0, 1.0, 0.0).astype(BF)


def hiding(bias, img_rows):
    return jnp.concatenate([jnp.zeros((img_rows, 128), BF), bias], axis=0)


def biased(ref, bias, cols):
    return jnp.concatenate([ref[0, :, cols], bias], axis=1)


def summed(ref, cols):
    return jnp.concatenate([ref[1, :, cols], jnp.ones((ref.shape[1], 128), BF)], axis=1)


def own_kernel(bias_ref, q_ref, kv_ref, top_ref, sum_ref, out_ref):
    rows, part = q_ref.shape
    count = rows // 2
    bias = hiding(bias_ref[0], rows - bias_ref.shape[1])
    lane, one_lane = lane_masks(count)
    for col in range(0, part, 128):
        cols = slice(col, col + 128)
        key, value = biased(kv_ref, bias, cols), summed(kv_ref, cols)
        for start in range(0, rows, count):
            span = slice(start, start + count)
            tops, sums, outs = [], [], []
            for head in range(2):
                score = head_scores(q_ref[span, cols], [key], lane, one_lane, head)[0]
                top = jnp.max(score, axis=-1, keepdims=True)
                both = dot(jnp.exp(score - top).astype(BF), value)
                tops.append(top)
                outs.append(both[:, :128])
                sums.append(both[:, 128:])
            top_ref[span, cols] = both_halves(tops, lane)
            sum_ref[span, cols] = both_halves(sums, lane)
            out_ref[span, cols] = both_halves(outs, lane)


def own_call(bias, query, keys):
    shape = jax.ShapeDtypeStruct(query.shape, F32)
    return pl.pallas_call(
        own_kernel,
        out_shape=[shape] * 3,
        in_specs=[VM] * 3,
        out_specs=[VM] * 3,
        compiler_params=pltpu.CompilerParams(vmem_limit_bytes=VMEM_LIMIT),
        cost_estimate=COST,
        name="attend_own",
    )(bias, query, keys)


def attend_kernel(start, counts, gate_rows, *refs):
    groups = len(counts)
    count = sum(counts)
    mods, bias_ref, q_ref, top_ref, sum_ref, out_ref, kv_ref = refs[:7]
    w_refs = refs[7 : 7 + groups]
    part = q_ref.shape[1]
    lane, one_lane = lane_masks(count)
    bias = hiding(bias_ref[1], kv_ref.shape[1] - bias_ref.shape[1])
    span = slice(start, start + count)
    att = []
    for col in range(0, part, 128):
        cols = slice(col, col + 128)
        key, val = biased(kv_ref, bias, cols), summed(kv_ref, cols)
        outs, sums, scales = [], [], []
        for head in range(2):
            score = head_scores(q_ref[span, cols], [key], lane, one_lane, head)[0]
            before = top_ref[span, col + 64 * head : col + 64 * head + 1]
            top = jnp.maximum(before, jnp.max(score, axis=-1, keepdims=True))
            both = dot(jnp.exp(score - top).astype(BF), val)
            outs.append(both[:, :128])
            sums.append(both[:, 128:])
            scales.append(jnp.exp(before - top))
        scale = both_halves(scales, lane)
        total = both_halves(sums, lane) + scale * sum_ref[span, cols]
        att.append(((both_halves(outs, lane) + scale * out_ref[span, cols]) / total).astype(BF))
    att = jnp.concatenate(att, axis=1)
    first = 0
    for i, (rows, row) in enumerate(zip(counts, gate_rows)):
        outs = refs[7 + groups + 2 * i : 9 + groups + 2 * i]
        project_out(att[first : first + rows], mods[row : row + 1, :], w_refs[i], *outs)
        first += rows


def project_out(left, gate, w_ref, keep_ref, send_ref):
    blk = lax.axis_index("blk")
    part = keep_ref.shape[2]
    width = gate.shape[1]
    for pair in range(2):
        which = (blk >> 1) ^ pair
        value = dot(left, w_ref[:, pl.ds(pl.multiple_of(which * 2 * part, 2 * part), 2 * part)])
        value = value * jnp.where(which == 0, gate[:, : width // 2], gate[:, width // 2 :])
        low, high = value[:, :part].astype(BF), value[:, part:].astype(BF)

        @pl.when((blk & 1) == 0)
        def _():
            keep_ref[pair] = low
            send_ref[pair] = high

        @pl.when((blk & 1) == 1)
        def _():
            keep_ref[pair] = high
            send_ref[pair] = low


def attend_call(mods, bias, query, state, keys, start, counts, gate_rows, weights):
    shapes = []
    for count in counts:
        shapes += [jax.ShapeDtypeStruct((2, count, query.shape[1]), BF)] * 2
    return pl.pallas_call(
        functools.partial(attend_kernel, start, counts, gate_rows),
        out_shape=shapes,
        in_specs=[VM] * (7 + len(weights)),
        out_specs=[VM] * len(shapes),
        compiler_params=pltpu.CompilerParams(vmem_limit_bytes=VMEM_LIMIT),
        cost_estimate=COST,
        name="attend",
    )(mods, bias, query, *state, keys, *weights)


def mlp_kernel(mods, mine, near, up_ref, down_ref, keep_ref, send_ref, raw_ref, acts_ref):
    blk = lax.axis_index("blk")
    rows, part = mine.shape[1:]
    span = up_ref.shape[1] // 3
    for j in range(4):
        value = (near if j & 1 else mine)[j >> 1]
        raw_ref[:, pl.ds(pl.multiple_of((blk ^ j) * part, part), part)] = value
    norm_rows(raw_ref, acts_ref, 0, rows, mods[3:4, :], mods[4:5, :])
    for i in range(3):
        cols = slice(i * span, i * span + span)
        hidden = dot(acts_ref[...], up_ref[:, cols])
        raw_ref[:, cols] = jax.nn.gelu(hidden, approximate=True).astype(BF)
    project_out(raw_ref[...], mods[5:6, :], down_ref, keep_ref, send_ref)


def mlp_call(mods, mine, near, up, down):
    rows, part = mine.shape[1:]
    shape = jax.ShapeDtypeStruct((2, rows, part), BF)
    return pl.pallas_call(
        mlp_kernel,
        out_shape=[shape, shape],
        in_specs=[VM] * 5,
        out_specs=[VM, VM],
        scratch_shapes=[pltpu.VMEM((rows, 4 * part), BF)] * 2,
        compiler_params=pltpu.CompilerParams(vmem_limit_bytes=VMEM_LIMIT),
        cost_estimate=COST,
        name="mlp",
    )(mods, mine, near, up, down)


def swap(values, axis, size, bit):
    return lax.ppermute(values, axis, [(i, i ^ bit) for i in range(size)])


def after(value, *others):
    return lax.optimization_barrier((value, *others))[0]


def add(*terms):
    return sum(term.astype(F32) for term in terms).astype(BF)


def small_call(kernel, name, outs, args, scratch=(), spec=VM):
    return pl.pallas_call(
        kernel,
        out_shape=[jax.ShapeDtypeStruct(shape, BF) for shape in outs],
        in_specs=[spec] * len(args),
        out_specs=[VM] * len(outs),
        scratch_shapes=list(scratch),
        compiler_params=pltpu.CompilerParams(vmem_limit_bytes=VMEM_LIMIT),
        cost_estimate=COST,
        name=name,
    )(*args)


def pack_kernel(image, text, out_ref, slots_ref, text_ref, sems):
    requests, image_rows, part = image.shape
    copies = fetch((text, image), (text_ref, out_ref.at[:, :image_rows, :]), sems)
    copies[0].wait()
    slots_ref[...] = jnp.zeros_like(slots_ref)
    for slot in range(text_ref.shape[0]):
        value = text_ref[slot].astype(F32)
        for i in range(part // 128):
            slots_ref[i, pl.ds(slot, requests, stride=TXT_PAD), :] = value[:, i * 128 : i * 128 + 128]
    for i in range(part // 128):
        piece = slots_ref[i].reshape(requests, TXT_PAD, 128).astype(BF)
        out_ref[:, image_rows:, i * 128 : i * 128 + 128] = piece
    copies[1].wait()


def sum_kernel(first, left_ref, right_ref, out_ref):
    for i in range(first, 2):
        out_ref[i - first] = add(left_ref[i], right_ref[i])


def away_kernel(image_ref, came_i, text_ref, came_t, out_ref):
    rows = image_ref.shape[1]
    out_ref[:rows, :] = add(image_ref[1], came_i[1])
    out_ref[rows:, :] = add(text_ref[1], came_t[1])


def core_sum(kept, came, first):
    shape = (2 - first,) + kept.shape[1:]
    return small_call(functools.partial(sum_kernel, first), "core_sum", [shape], [kept, came])[0]


def middle_kernel(begin, own_ref, far_ref, sum_ref, back_ref, out_ref):
    rows, part = out_ref.shape[1:]
    image_rows = own_ref.shape[1] - TXT_PAD
    for i, ref in enumerate((own_ref, far_ref)):
        start = ref[begin : begin + rows // image_rows, :image_rows, :].reshape(rows, part)
        out_ref[i] = add(start, sum_ref[i], back_ref[1 - i])


def first_kernel(own_ref, keep_t, came_t, mid_a, keep_a, came_a, last_a, image_ref, text_ref):
    rows = image_ref.shape[0]
    image_ref[...] = add(mid_a[0], keep_a[0], came_a[0], last_a[:rows, :])
    sources, slots, part = own_ref.shape
    total = keep_t[0].astype(F32) + came_t[0].astype(F32) + last_a[rows:, :].astype(F32)
    text = own_ref[:, slots - TXT_PAD :, :].astype(F32) + total.reshape(sources, TXT_PAD, part)
    text_ref[...] = text.astype(BF)


def final_kernel(image_ref, text_ref, mid_b, keep_b, came_b, last_b, out_ref):
    sources, slots, part = out_ref.shape
    image_rows = slots - TXT_PAD
    first = image_ref.shape[0] // image_rows
    out_ref[:first, :image_rows, :] = image_ref[...].reshape(first, image_rows, part)
    value = add(mid_b[0], keep_b[0], came_b[0], last_b[0])
    out_ref[first:, :image_rows, :] = value.reshape(sources - first, image_rows, part)
    out_ref[:, image_rows:, :] = text_ref[...]


def per_device(
    tiles,
    image_tokens,
    text_tokens,
    step_index,
    text_length,
    image_table,
    text_table,
    qkv_image,
    qkv_text,
    attn_out_image,
    attn_out_text,
    query_gain_image,
    key_gain_image,
    query_gain_text,
    key_gain_text,
    up_weight,
    down_weight,
):
    requests, image_rows, part = image_tokens.shape
    text_rows = text_tokens.shape[1]
    groups = [[t for t in range(tiles) if (t >> 1) & 1 == p] for p in (0, 1)]
    tables = [jnp.transpose(table, (1, 0, 2)) for table in (image_table, text_table)]
    weights = [jnp.transpose(weight, (1, 0, 2)) for weight in (qkv_image, qkv_text)]
    gains = [
        gain.reshape(1, HEAD_DIM)
        for gain in (query_gain_image, key_gain_image, query_gain_text, key_gain_text)
    ]

    slots = (requests, image_rows + TXT_PAD, part)
    text_slots = jnp.transpose(text_tokens, (1, 0, 2))
    packed = small_call(
        pack_kernel,
        "pack",
        [slots],
        pinned(image_tokens, text_slots),
        [
            pltpu.VMEM((part // 128, requests * TXT_PAD, 128), F32),
            pltpu.VMEM(text_slots.shape, BF),
            pltpu.SemaphoreType.DMA((2,)),
        ],
        HB,
    )[0]
    own = lax.all_to_all(packed, "tile", 0, 0, axis_index_groups=groups, tiled=True)
    far = swap(own, "blk", 4, 2)
    other = swap(own, "tile", tiles, 2)
    near = swap(own, "blk", 4, 1)
    mods, head_gains, bias, *wide = prep_call(after(step_index, own), text_length, tables, gains, weights)

    def tied(*others):
        return after(mods, *others)

    def project(mods, pieces, parts):
        return qkv_call(mods, head_gains, pieces, (0, 0, 0, 0), requests, wide, parts)

    far = after(far, mods)
    other = after(other, far)
    other_far = swap(other, "blk", 4, 2)
    diag = swap(far, "blk", 4, 1)
    query, mine = project(mods, [own, near, far, diag], PARTS)
    other_near = swap(after(other, query), "blk", 4, 1)
    state = own_call(bias, query, mine)
    other_far = after(other_far, state[0])
    other_diag = swap(other_far, "blk", 4, 1)
    keys = project(tied(state[0]), [other, other_near, other_far, other_diag], PARTS[:2])[0]

    first = requests * 10 // 16
    rows_a, rows_b = first * image_rows, (requests - first) * image_rows
    txt_rows = requests * TXT_PAD

    def attend(mods, *groups):
        return attend_call(mods, bias, query, state, keys, *groups)

    def middle(begin, sums, back):
        args = [own, far, sums, back]
        return small_call(functools.partial(middle_kernel, begin), "middle", [sums.shape], args)[0]

    keep_a, send_a = attend(mods, 0, (rows_a,), (2,), (attn_out_image,))
    came_a = swap(send_a, "blk", 4, 1)
    sum_a = core_sum(keep_a, came_a, 0)
    back_a = swap(sum_a, "blk", 4, 2)
    keep_b, send_b, keep_t, send_t = attend(
        tied(sum_a), rows_a, (rows_b, txt_rows), (2, 10), (attn_out_image, attn_out_text)
    )
    came_b = swap(send_b, "blk", 4, 1)
    sum_b = core_sum(keep_b, came_b, 0)
    mid_a = middle(0, sum_a, after(back_a, sum_b))
    near_a = swap(mid_a, "blk", 4, 1)
    back_b = swap(sum_b, "blk", 4, 2)
    came_t = swap(send_t, "blk", 4, 1)
    came_t = after(came_t, sum_b)
    down_a, send_a = mlp_call(tied(came_t), mid_a, near_a, up_weight, down_weight)
    came_a = swap(send_a, "blk", 4, 1)
    mid_b = middle(first, sum_b, after(back_b, down_a))
    near_b = swap(mid_b, "blk", 4, 1)
    args = [after(down_a, near_b), came_a, keep_t, came_t]
    away_a = small_call(away_kernel, "away", [(rows_a + txt_rows, part)], args)[0]
    last_a = swap(away_a, "blk", 4, 2)
    down_b, send_b = mlp_call(tied(away_a), mid_b, near_b, up_weight, down_weight)
    args = [own, keep_t, came_t, mid_a, down_a, came_a, after(last_a, down_b)]
    image_a, text_out = small_call(
        first_kernel, "first", [(rows_a, part), (requests, TXT_PAD, part)], args
    )
    came_b = swap(send_b, "blk", 4, 1)
    away_b = core_sum(after(down_b, image_a), came_b, 1)
    last_b = swap(away_b, "blk", 4, 2)

    args = [image_a, text_out, mid_b, down_b, came_b, last_b]
    result = small_call(final_kernel, "final", [slots], args)[0]
    result = lax.all_to_all(result, "tile", 0, 0, axis_index_groups=groups, tiled=True)
    return (result[:, :image_rows], result[:, image_rows : image_rows + text_rows])


def solution(mesh):
    in_specs = (
        P(None, "tile", "blk"),
        P(None, "tile", "blk"),
        P(),
        P(),
        P(),
        P(),
        P(None, None, "blk"),
        P(None, None, "blk"),
        P("blk", None),
        P("blk", None),
        P(),
        P(),
        P(),
        P(),
        P(None, "blk"),
        P("blk", None),
    )
    out_specs = (P(None, "tile", "blk"), P(None, "tile", "blk"))
    return jax.shard_map(
        functools.partial(per_device, mesh.shape["tile"]),
        mesh=mesh,
        in_specs=in_specs,
        out_specs=out_specs,
        check_vma=False,
    )
```

```python
import functools

import jax
import jax.numpy as jnp
from jax import lax
from jax.experimental import pallas as pl
from jax.experimental.pallas import tpu as pltpu
from jax.sharding import PartitionSpec as P

HEAD_DIM = 64
BF = jnp.bfloat16
F32 = jnp.float32
HIDDEN_BIAS = -32768.0
TXT_PAD = 8
PARTS = (1, 2, 0)
VMEM_LIMIT = 28 << 20
VM = pl.BlockSpec(memory_space=pltpu.VMEM)
SM = pl.BlockSpec(memory_space=pltpu.SMEM)
HB = pl.BlockSpec(memory_space=pltpu.HBM)
COST = pl.CostEstimate(flops=1, transcendentals=0, bytes_accessed=1)


def dot(left, right):
    return jnp.dot(left, right, preferred_element_type=F32)


def dot_t(left, right):
    return lax.dot_general(left, right, (((1,), (1,)), ((), ())), preferred_element_type=F32)


def pinned(*arrays):
    return [pltpu.with_memory_space_constraint(array, pltpu.HBM) for array in arrays]


def fetch(sources, targets, sems):
    copies = [
        pltpu.make_async_copy(source, target, sems.at[i])
        for i, (source, target) in enumerate(zip(sources, targets))
    ]
    for copy in copies:
        copy.start()
    return copies


def table_row(table_ref, step, row):
    plane = table_ref[row].astype(F32)
    here = lax.broadcasted_iota(jnp.int32, plane.shape, 0) == step
    return jnp.sum(jnp.where(here, plane, 0.0), axis=0, keepdims=True)


def prep_kernel(step_ref, length_ref, *refs):
    mods_ref, gains_ref, bias_ref, wimg_ref, wtxt_ref = refs[8:13]
    part = refs[6].shape[2]
    sources, targets = list(refs[:6]), list(refs[13:19])
    for w, w_ref in zip(refs[6:8], (wimg_ref, wtxt_ref)):
        for i, which in enumerate(PARTS):
            sources.append(w.at[which])
            targets.append(w_ref.at[:, i * part : (i + 1) * part])
    copies = fetch(sources, targets, refs[19])
    for copy in copies[:6]:
        copy.wait()
    itab, ttab, gqi, gki, gqt, gkt = refs[13:19]
    tile = lax.axis_index("tile")
    request = (tile >> 2) * 2 + (tile & 1)
    step, length = step_ref[request], length_ref[request]
    for row in range(6):
        mods_ref[row : row + 1, :] = table_row(itab, step, row)
    for row in range(3):
        mods_ref[8 + row : 9 + row, :] = table_row(ttab, step, row)
    for row, ref in enumerate((gqi, gki, gqt, gkt)):
        gains_ref[row : row + 1, :] = jnp.concatenate([ref[...], ref[...]], axis=1)
    inner = lax.broadcasted_iota(jnp.int32, bias_ref.shape[1:], 0)
    source, slot = inner >> 3, inner & 7
    for side in range(2):
        parity = ((tile >> 1) & 1) ^ side
        sender = (source >> 1) * 4 + parity * 2 + (source & 1)
        seen = (slot < 5) & (sender * 5 + slot < length)
        bias_ref[side] = jnp.where(seen, 0.0, HIDDEN_BIAS).astype(BF)
    for copy in copies[6:]:
        copy.wait()


def prep_call(step_index, text_length, tables, gains, weights):
    width = tables[0].shape[2]
    wide = jax.ShapeDtypeStruct((width, 3 * weights[0].shape[2]), BF)
    return pl.pallas_call(
        prep_kernel,
        out_shape=[
            jax.ShapeDtypeStruct((16, width), F32),
            jax.ShapeDtypeStruct((8, 128), F32),
            jax.ShapeDtypeStruct((2, 128, 128), BF),
            wide,
            wide,
        ],
        in_specs=[SM, SM] + [HB] * 8,
        out_specs=[VM] * 5,
        scratch_shapes=[pltpu.VMEM(x.shape, x.dtype) for x in (*tables, *gains)]
        + [pltpu.SemaphoreType.DMA((12,))],
        compiler_params=pltpu.CompilerParams(vmem_limit_bytes=VMEM_LIMIT),
        cost_estimate=COST,
        name="prep",
    )(step_index, text_length, *pinned(*tables, *gains, *weights))


def norm_rows(raw_ref, acts_ref, start, count, shift, scale, block=32):
    width = raw_ref.shape[1]
    gain = 1.0 + scale

    def body(i, carry):
        rows = pl.ds(pl.multiple_of(start + i * block, block), block)
        values = raw_ref[rows, :].astype(F32)
        centre = jnp.sum(values, axis=-1, keepdims=True) * (1.0 / width)
        moved = values - centre
        spread = jnp.sum(moved * moved, axis=-1, keepdims=True) * (1.0 / width)
        acts_ref[rows, :] = (moved * lax.rsqrt(spread + 1e-06) * gain + shift).astype(BF)
        return carry

    lax.fori_loop(0, count // block, body, 0, unroll=True)


def head_scale(values, group):
    parts = []
    for col in range(0, values.shape[1], 128):
        piece = values[:, col : col + 128]
        squares = piece * piece
        high = squares.astype(BF)
        low = (squares - high.astype(F32)).astype(BF)
        parts.append(dot(jnp.concatenate([high, low], axis=1), group))
    return lax.rsqrt(jnp.concatenate(parts, axis=1) + 1e-06)


def group_matrix():
    row = lax.broadcasted_iota(jnp.int32, (256, 128), 0)
    col = lax.broadcasted_iota(jnp.int32, (256, 128), 1)
    same = ((row & 127) >> 6) == (col >> 6)
    return jnp.where(same, 1.0 / HEAD_DIM, 0.0).astype(BF)


def qkv_kernel(begin, sources, parts, *refs):
    mods, gains, x0, x1, x2, x3, wimg_ref, wtxt_ref = refs[:8]
    outs, (raw_ref, acts_ref) = refs[8:-2], refs[-2:]
    blk = lax.axis_index("blk")
    part = x0.shape[2]
    image_rows = x0.shape[1] - TXT_PAD
    img, txt = sources * image_rows, sources * TXT_PAD
    for j, (ref, first) in enumerate(zip((x0, x1, x2, x3), begin)):
        cols = pl.ds(pl.multiple_of((blk ^ j) * part, part), part)
        raw_ref[:img, cols] = ref[first : first + sources, :image_rows, :].reshape(img, part)
        text = ref[first : first + sources, image_rows:, :].astype(F32).reshape(txt, part)
        raw_ref[img:, cols] = text.astype(BF)
    norm_rows(raw_ref, acts_ref, img, txt, mods[8:9, :], mods[9:10, :])
    norm_rows(raw_ref, acts_ref, 0, img, mods[0:1, :], mods[1:2, :])
    group = group_matrix()
    kv_ref = outs[-1]
    for w_ref, first, last, row in ((wtxt_ref, img, img + txt, 2), (wimg_ref, 0, img, 0)):
        projected = dot(acts_ref[first:last, :], w_ref[:, : len(parts) * part])
        for i, which in enumerate(parts):
            values = projected[:, i * part : (i + 1) * part]
            if which == 2:
                kv_ref[1, first:last, :] = values.astype(BF)
                continue
            gain = jnp.concatenate([gains[row + which : row + which + 1, :]] * (part // 128), axis=1)
            normed = (values * head_scale(values, group) * gain).astype(BF)
            if which == 1:
                kv_ref[0, first:last, :] = normed
            else:
                outs[0][first:last, :] = normed * BF(HEAD_DIM**-0.5)


def qkv_call(mods, gains, pieces, begin, sources, weights, parts):
    part = pieces[0].shape[2]
    rows, width = sources * pieces[0].shape[1], 4 * part
    outs = [jax.ShapeDtypeStruct((2, rows, part), BF)]
    if 0 in parts:
        outs = [jax.ShapeDtypeStruct((rows, part), BF)] + outs
    return pl.pallas_call(
        functools.partial(qkv_kernel, begin, sources, parts),
        out_shape=outs,
        in_specs=[VM] * 8,
        out_specs=[VM] * len(outs),
        scratch_shapes=[pltpu.VMEM((rows, width), BF)] * 2,
        compiler_params=pltpu.CompilerParams(vmem_limit_bytes=VMEM_LIMIT),
        cost_estimate=COST,
        name="qkv",
    )(mods, gains, *pieces, *weights)


def head_scores(query, keys, lane, one_lane, head):
    mine = (lane < 64) if head == 0 else (lane >= 64)
    left = jnp.concatenate([jnp.where(mine, query, BF(0.0)), one_lane], axis=1)
    return [dot_t(left, key) for key in keys]


def both_halves(values, lane):
    return jnp.where(lane < 64, values[0], values[1])


def lane_masks(rows):
    lane = lax.broadcasted_iota(jnp.int32, (rows, 128), 1)
    return lane, jnp.where(lane == 0, 1.0, 0.0).astype(BF)


def hiding(bias, img_rows):
    return jnp.concatenate([jnp.zeros((img_rows, 128), BF), bias], axis=0)


def biased(ref, bias, cols):
    return jnp.concatenate([ref[0, :, cols], bias], axis=1)


def summed(ref, cols):
    return jnp.concatenate([ref[1, :, cols], jnp.ones((ref.shape[1], 128), BF)], axis=1)


def own_kernel(bias_ref, q_ref, kv_ref, top_ref, sum_ref, out_ref):
    rows, part = q_ref.shape
    count = rows // 2
    bias = hiding(bias_ref[0], rows - bias_ref.shape[1])
    lane, one_lane = lane_masks(count)
    for col in range(0, part, 128):
        cols = slice(col, col + 128)
        key, value = biased(kv_ref, bias, cols), summed(kv_ref, cols)
        for start in range(0, rows, count):
            span = slice(start, start + count)
            tops, sums, outs = [], [], []
            for head in range(2):
                score = head_scores(q_ref[span, cols], [key], lane, one_lane, head)[0]
                top = jnp.max(score, axis=-1, keepdims=True)
                both = dot(jnp.exp(score - top).astype(BF), value)
                tops.append(top)
                outs.append(both[:, :128])
                sums.append(both[:, 128:])
            top_ref[span, cols] = both_halves(tops, lane)
            sum_ref[span, cols] = both_halves(sums, lane)
            out_ref[span, cols] = both_halves(outs, lane)


def own_call(bias, query, keys):
    shape = jax.ShapeDtypeStruct(query.shape, F32)
    return pl.pallas_call(
        own_kernel,
        out_shape=[shape] * 3,
        in_specs=[VM] * 3,
        out_specs=[VM] * 3,
        compiler_params=pltpu.CompilerParams(vmem_limit_bytes=VMEM_LIMIT),
        cost_estimate=COST,
        name="attend_own",
    )(bias, query, keys)


def attend_kernel(start, counts, gate_rows, *refs):
    groups = len(counts)
    count = sum(counts)
    mods, bias_ref, q_ref, top_ref, sum_ref, out_ref, kv_ref = refs[:7]
    w_refs = refs[7 : 7 + groups]
    part = q_ref.shape[1]
    lane, one_lane = lane_masks(count)
    bias = hiding(bias_ref[1], kv_ref.shape[1] - bias_ref.shape[1])
    span = slice(start, start + count)
    att = []
    for col in range(0, part, 128):
        cols = slice(col, col + 128)
        key, val = biased(kv_ref, bias, cols), summed(kv_ref, cols)
        outs, sums, scales = [], [], []
        for head in range(2):
            score = head_scores(q_ref[span, cols], [key], lane, one_lane, head)[0]
            before = top_ref[span, col + 64 * head : col + 64 * head + 1]
            top = jnp.maximum(before, jnp.max(score, axis=-1, keepdims=True))
            both = dot(jnp.exp(score - top).astype(BF), val)
            outs.append(both[:, :128])
            sums.append(both[:, 128:])
            scales.append(jnp.exp(before - top))
        scale = both_halves(scales, lane)
        total = both_halves(sums, lane) + scale * sum_ref[span, cols]
        att.append(((both_halves(outs, lane) + scale * out_ref[span, cols]) / total).astype(BF))
    att = jnp.concatenate(att, axis=1)
    first = 0
    for i, (rows, row) in enumerate(zip(counts, gate_rows)):
        outs = refs[7 + groups + 2 * i : 9 + groups + 2 * i]
        keep_ref, send_ref = outs
        sends = (send_ref.at[0], send_ref.at[1])
        project_out(att[first : first + rows], mods[row : row + 1, :], w_refs[i], keep_ref, sends)
        first += rows


def project_out(left, gate, w_ref, keep_ref, sends):
    blk = lax.axis_index("blk")
    part = keep_ref.shape[2]
    width = gate.shape[1]
    for pair in range(2):
        which = (blk >> 1) ^ pair
        value = dot(left, w_ref[:, pl.ds(pl.multiple_of(which * 2 * part, 2 * part), 2 * part)])
        value = value * jnp.where(which == 0, gate[:, : width // 2], gate[:, width // 2 :])
        low, high = value[:, :part].astype(BF), value[:, part:].astype(BF)

        @pl.when((blk & 1) == 0)
        def _():
            keep_ref[pair] = low
            sends[pair][...] = high

        @pl.when((blk & 1) == 1)
        def _():
            keep_ref[pair] = high
            sends[pair][...] = low


def attend_call(mods, bias, query, state, keys, start, counts, gate_rows, weights):
    shapes = []
    for count in counts:
        shapes += [jax.ShapeDtypeStruct((2, count, query.shape[1]), BF)] * 2
    return pl.pallas_call(
        functools.partial(attend_kernel, start, counts, gate_rows),
        out_shape=shapes,
        in_specs=[VM] * (7 + len(weights)),
        out_specs=[VM] * len(shapes),
        compiler_params=pltpu.CompilerParams(vmem_limit_bytes=VMEM_LIMIT),
        cost_estimate=COST,
        name="attend",
    )(mods, bias, query, *state, keys, *weights)


def mlp_kernel(mods, m0, m1, n0, n1, up_ref, down_ref, keep_ref, s0, s1, raw_ref, acts_ref):
    blk = lax.axis_index("blk")
    rows, part = m0.shape
    span = up_ref.shape[1] // 3
    for j in range(4):
        value = (m0, n0, m1, n1)[j][...]
        raw_ref[:, pl.ds(pl.multiple_of((blk ^ j) * part, part), part)] = value
    norm_rows(raw_ref, acts_ref, 0, rows, mods[3:4, :], mods[4:5, :])
    for i in range(3):
        cols = slice(i * span, i * span + span)
        hidden = dot(acts_ref[...], up_ref[:, cols])
        raw_ref[:, cols] = jax.nn.gelu(hidden, approximate=True).astype(BF)
    project_out(raw_ref[...], mods[5:6, :], down_ref, keep_ref, (s0, s1))


def mlp_call(mods, mine, near, up, down):
    rows, part = mine[0].shape
    kept = jax.ShapeDtypeStruct((2, rows, part), BF)
    sent = jax.ShapeDtypeStruct((rows, part), BF)
    return pl.pallas_call(
        mlp_kernel,
        out_shape=[kept, sent, sent],
        in_specs=[VM] * 7,
        out_specs=[VM] * 3,
        scratch_shapes=[pltpu.VMEM((rows, 4 * part), BF)] * 2,
        compiler_params=pltpu.CompilerParams(vmem_limit_bytes=VMEM_LIMIT),
        cost_estimate=COST,
        name="mlp",
    )(mods, *mine, *near, up, down)


def swap(values, axis, size, bit):
    return lax.ppermute(values, axis, [(i, i ^ bit) for i in range(size)])


def after(value, *others):
    return lax.optimization_barrier((value, *others))[0]


def add(*terms):
    return sum(term.astype(F32) for term in terms).astype(BF)


def small_call(kernel, name, outs, args, scratch=(), spec=VM):
    return pl.pallas_call(
        kernel,
        out_shape=[jax.ShapeDtypeStruct(shape, BF) for shape in outs],
        in_specs=[spec] * len(args),
        out_specs=[VM] * len(outs),
        scratch_shapes=list(scratch),
        compiler_params=pltpu.CompilerParams(vmem_limit_bytes=VMEM_LIMIT),
        cost_estimate=COST,
        name=name,
    )(*args)


def pack_kernel(image, text, out_ref, slots_ref, text_ref, sems):
    requests, image_rows, part = image.shape
    copies = fetch((text, image), (text_ref, out_ref.at[:, :image_rows, :]), sems)
    copies[0].wait()
    slots_ref[...] = jnp.zeros_like(slots_ref)
    for slot in range(text_ref.shape[0]):
        value = text_ref[slot].astype(F32)
        for i in range(part // 128):
            slots_ref[i, pl.ds(slot, requests, stride=TXT_PAD), :] = value[:, i * 128 : i * 128 + 128]
    for i in range(part // 128):
        piece = slots_ref[i].reshape(requests, TXT_PAD, 128).astype(BF)
        out_ref[:, image_rows:, i * 128 : i * 128 + 128] = piece
    copies[1].wait()


def sum_kernel(left_ref, right_ref, out_ref):
    for i in range(2):
        out_ref[i] = add(left_ref[i], right_ref[i])


def joint_kernel(left_ref, right_ref, text_ref, came_t, image_ref, out_ref):
    rows = image_ref.shape[1]
    text = add(text_ref[1], came_t[1])
    half = text.shape[0] // 2
    for i in range(2):
        value = add(left_ref[i], right_ref[i])
        image_ref[i] = value
        out_ref[i, :rows, :] = value
        out_ref[i, rows:, :] = text[i * half : i * half + half]


def middle_kernel(begin, own_ref, far_ref, sum_ref, back_ref, *outs):
    rows, part = sum_ref.shape[1:]
    image_rows = own_ref.shape[1] - TXT_PAD
    for i, (ref, out_ref) in enumerate(zip((own_ref, far_ref), outs)):
        start = ref[begin : begin + rows // image_rows, :image_rows, :].reshape(rows, part)
        out_ref[...] = add(start, sum_ref[i], back_ref[1 - i, :rows, :])


def away_kernel(keep_ref, came_ref, out_ref):
    out_ref[...] = add(keep_ref[1], came_ref[...])


def first_kernel(own_ref, keep_t, came_t, back_b, mid_a, keep_a, came_a, last_a, image_ref, text_ref):
    image_ref[...] = add(mid_a[...], keep_a[0], came_a[...], last_a[...])
    sources, slots, part = own_ref.shape
    rows = back_b.shape[1] - keep_t.shape[1] // 2
    back = jnp.concatenate([back_b[0, rows:, :], back_b[1, rows:, :]], axis=0)
    total = keep_t[0].astype(F32) + came_t[0].astype(F32) + back.astype(F32)
    text = own_ref[:, slots - TXT_PAD :, :].astype(F32) + total.reshape(sources, TXT_PAD, part)
    text_ref[...] = text.astype(BF)


def final_kernel(image_ref, text_ref, mid_b, keep_b, came_b, last_b, out_ref):
    sources, slots, part = out_ref.shape
    image_rows = slots - TXT_PAD
    first = image_ref.shape[0] // image_rows
    out_ref[:first, :image_rows, :] = image_ref[...].reshape(first, image_rows, part)
    value = add(mid_b[...], keep_b[0], came_b[...], last_b[...])
    out_ref[first:, :image_rows, :] = value.reshape(sources - first, image_rows, part)
    out_ref[:, image_rows:, :] = text_ref[...]


def per_device(
    tiles,
    image_tokens,
    text_tokens,
    step_index,
    text_length,
    image_table,
    text_table,
    qkv_image,
    qkv_text,
    attn_out_image,
    attn_out_text,
    query_gain_image,
    key_gain_image,
    query_gain_text,
    key_gain_text,
    up_weight,
    down_weight,
):
    requests, image_rows, part = image_tokens.shape
    text_rows = text_tokens.shape[1]
    groups = [[t for t in range(tiles) if (t >> 1) & 1 == p] for p in (0, 1)]
    tables = [jnp.transpose(table, (1, 0, 2)) for table in (image_table, text_table)]
    weights = [jnp.transpose(weight, (1, 0, 2)) for weight in (qkv_image, qkv_text)]
    gains = [
        gain.reshape(1, HEAD_DIM)
        for gain in (query_gain_image, key_gain_image, query_gain_text, key_gain_text)
    ]

    slots = (requests, image_rows + TXT_PAD, part)
    text_slots = jnp.transpose(text_tokens, (1, 0, 2))
    packed = small_call(
        pack_kernel,
        "pack",
        [slots],
        pinned(image_tokens, text_slots),
        [
            pltpu.VMEM((part // 128, requests * TXT_PAD, 128), F32),
            pltpu.VMEM(text_slots.shape, BF),
            pltpu.SemaphoreType.DMA((2,)),
        ],
        HB,
    )[0]
    own = lax.all_to_all(packed, "tile", 0, 0, axis_index_groups=groups, tiled=True)
    far = swap(own, "blk", 4, 2)
    other = swap(own, "tile", tiles, 2)
    own_near = swap(own, "blk", 4, 1)
    mods, head_gains, bias, *wide = prep_call(after(step_index, own), text_length, tables, gains, weights)

    def tied(*others):
        return after(mods, *others)

    def project(mods, pieces, parts):
        return qkv_call(mods, head_gains, pieces, (0, 0, 0, 0), requests, wide, parts)

    far = after(far, mods)
    other = after(other, far)
    other_far = swap(other, "blk", 4, 2)
    diag = swap(far, "blk", 4, 1)
    query, mine = project(mods, [own, own_near, far, diag], PARTS)
    other_near = swap(after(other, query), "blk", 4, 1)
    state = own_call(bias, query, mine)
    other_far = after(other_far, state[0])
    other_diag = swap(other_far, "blk", 4, 1)
    keys = project(tied(state[0]), [other, other_near, other_far, other_diag], PARTS[:2])[0]

    first = requests * 10 // 16
    rows_a, rows_b = first * image_rows, (requests - first) * image_rows
    txt_rows = requests * TXT_PAD

    def attend(mods, *groups):
        return attend_call(mods, bias, query, state, keys, *groups)

    def middle(begin, sums, back):
        kernel = functools.partial(middle_kernel, begin)
        return small_call(kernel, "middle", [sums.shape[1:]] * 2, [own, far, sums, back])

    def near(value):
        return swap(value, "blk", 4, 1)

    def across(value):
        return swap(value, "blk", 4, 2)

    def away(kept, came):
        return small_call(away_kernel, "away", [came.shape], [kept, came])[0]

    keep_a, send_a = attend(mods, 0, (rows_a,), (2,), (attn_out_image,))
    sum_a = small_call(sum_kernel, "core_sum", [keep_a.shape], [keep_a, near(send_a)])[0]
    back_a = across(sum_a)
    keep_b, send_b, keep_t, send_t = attend(
        tied(sum_a), rows_a, (rows_b, txt_rows), (2, 10), (attn_out_image, attn_out_text)
    )
    came_t = near(send_t)
    shapes = [keep_b.shape, (2, rows_b + txt_rows // 2, part)]
    sum_b, joint = small_call(joint_kernel, "joint", shapes, [keep_b, near(send_b), keep_t, came_t])
    back_b = across(joint)
    mid_a = middle(0, sum_a, after(back_a, sum_b))
    near_a = [near(value) for value in mid_a]

    down_a, *send_a = mlp_call(mods, mid_a, near_a, up_weight, down_weight)
    came_a = [near(value) for value in send_a]
    mid_b = middle(first, sum_b, after(back_b, down_a))
    near_b = [near(value) for value in mid_b]
    away_a = away(after(down_a, *near_b), came_a[1])
    last_a = across(away_a)
    down_b, *send_b = mlp_call(tied(away_a), mid_b, near_b, up_weight, down_weight)
    args = [own, keep_t, came_t, back_b, mid_a[0], down_a, came_a[0], after(last_a, down_b)]
    image_a, text_out = small_call(
        first_kernel, "first", [(rows_a, part), (requests, TXT_PAD, part)], args
    )
    came_b = [near(value) for value in send_b]
    away_b = away(after(down_b, image_a), came_b[1])
    last_b = across(away_b)

    args = [image_a, text_out, mid_b[0], down_b, came_b[0], last_b]
    result = small_call(final_kernel, "final", [slots], args)[0]
    result = lax.all_to_all(result, "tile", 0, 0, axis_index_groups=groups, tiled=True)
    return (result[:, :image_rows], result[:, image_rows : image_rows + text_rows])


def solution(mesh):
    in_specs = (
        P(None, "tile", "blk"),
        P(None, "tile", "blk"),
        P(),
        P(),
        P(),
        P(),
        P(None, None, "blk"),
        P(None, None, "blk"),
        P("blk", None),
        P("blk", None),
        P(),
        P(),
        P(),
        P(),
        P(None, "blk"),
        P("blk", None),
    )
    out_specs = (P(None, "tile", "blk"), P(None, "tile", "blk"))
    return jax.shard_map(
        functools.partial(per_device, mesh.shape["tile"]),
        mesh=mesh,
        in_specs=in_specs,
        out_specs=out_specs,
        check_vma=False,
    )
```

```python
import functools

import jax
import jax.numpy as jnp
from jax import lax
from jax.experimental import pallas as pl
from jax.experimental.pallas import tpu as pltpu
from jax.sharding import PartitionSpec as P

HEAD_DIM = 64
BF = jnp.bfloat16
F32 = jnp.float32
HIDDEN_BIAS = -32768.0
TXT_PAD = 8
PARTS = (1, 2, 0)
VMEM_LIMIT = 28 << 20
VM = pl.BlockSpec(memory_space=pltpu.VMEM)
SM = pl.BlockSpec(memory_space=pltpu.SMEM)
HB = pl.BlockSpec(memory_space=pltpu.HBM)
COST = pl.CostEstimate(flops=1, transcendentals=0, bytes_accessed=1)


def dot(left, right):
    return jnp.dot(left, right, preferred_element_type=F32)


def dot_t(left, right):
    return lax.dot_general(left, right, (((1,), (1,)), ((), ())), preferred_element_type=F32)


def pinned(*arrays):
    return [pltpu.with_memory_space_constraint(array, pltpu.HBM) for array in arrays]


def fetch(sources, targets, sems):
    copies = [
        pltpu.make_async_copy(source, target, sems.at[i])
        for i, (source, target) in enumerate(zip(sources, targets))
    ]
    for copy in copies:
        copy.start()
    return copies


def table_row(table_ref, step, row):
    plane = table_ref[row].astype(F32)
    here = lax.broadcasted_iota(jnp.int32, plane.shape, 0) == step
    return jnp.sum(jnp.where(here, plane, 0.0), axis=0, keepdims=True)


def prep_kernel(step_ref, length_ref, *refs):
    mods_ref, gains_ref, bias_ref, wimg_ref, wtxt_ref = refs[8:13]
    part = refs[6].shape[2]
    sources, targets = list(refs[:6]), list(refs[13:19])
    for w, w_ref in zip(refs[6:8], (wimg_ref, wtxt_ref)):
        for i, which in enumerate(PARTS):
            sources.append(w.at[which])
            targets.append(w_ref.at[:, i * part : (i + 1) * part])
    copies = fetch(sources, targets, refs[19])
    for copy in copies[:6]:
        copy.wait()
    itab, ttab, gqi, gki, gqt, gkt = refs[13:19]
    tile = lax.axis_index("tile")
    request = (tile >> 2) * 2 + (tile & 1)
    step, length = step_ref[request], length_ref[request]
    for row in range(6):
        mods_ref[row : row + 1, :] = table_row(itab, step, row)
    for row in range(3):
        mods_ref[8 + row : 9 + row, :] = table_row(ttab, step, row)
    for row, ref in enumerate((gqi, gki, gqt, gkt)):
        gains_ref[row : row + 1, :] = jnp.concatenate([ref[...], ref[...]], axis=1)
    inner = lax.broadcasted_iota(jnp.int32, bias_ref.shape[1:], 0)
    source, slot = inner >> 3, inner & 7
    for side in range(2):
        parity = ((tile >> 1) & 1) ^ side
        sender = (source >> 1) * 4 + parity * 2 + (source & 1)
        seen = (slot < 5) & (sender * 5 + slot < length)
        bias_ref[side] = jnp.where(seen, 0.0, HIDDEN_BIAS).astype(BF)
    for copy in copies[6:]:
        copy.wait()


def prep_call(step_index, text_length, tables, gains, weights):
    width = tables[0].shape[2]
    wide = jax.ShapeDtypeStruct((width, 3 * weights[0].shape[2]), BF)
    return pl.pallas_call(
        prep_kernel,
        out_shape=[
            jax.ShapeDtypeStruct((16, width), F32),
            jax.ShapeDtypeStruct((8, 128), F32),
            jax.ShapeDtypeStruct((2, 128, 128), BF),
            wide,
            wide,
        ],
        in_specs=[SM, SM] + [HB] * 8,
        out_specs=[VM] * 5,
        scratch_shapes=[pltpu.VMEM(x.shape, x.dtype) for x in (*tables, *gains)]
        + [pltpu.SemaphoreType.DMA((12,))],
        compiler_params=pltpu.CompilerParams(vmem_limit_bytes=VMEM_LIMIT),
        cost_estimate=COST,
        name="prep",
    )(step_index, text_length, *pinned(*tables, *gains, *weights))


def norm_rows(raw_ref, acts_ref, start, count, shift, scale, block=32):
    width = raw_ref.shape[1]
    gain = 1.0 + scale

    def body(i, carry):
        rows = pl.ds(pl.multiple_of(start + i * block, block), block)
        values = raw_ref[rows, :].astype(F32)
        centre = jnp.sum(values, axis=-1, keepdims=True) * (1.0 / width)
        moved = values - centre
        spread = jnp.sum(moved * moved, axis=-1, keepdims=True) * (1.0 / width)
        acts_ref[rows, :] = (moved * lax.rsqrt(spread + 1e-06) * gain + shift).astype(BF)
        return carry

    lax.fori_loop(0, count // block, body, 0, unroll=True)


def head_scale(values, group):
    parts = []
    for col in range(0, values.shape[1], 128):
        piece = values[:, col : col + 128]
        squares = piece * piece
        high = squares.astype(BF)
        low = (squares - high.astype(F32)).astype(BF)
        parts.append(dot(jnp.concatenate([high, low], axis=1), group))
    return lax.rsqrt(jnp.concatenate(parts, axis=1) + 1e-06)


def group_matrix():
    row = lax.broadcasted_iota(jnp.int32, (256, 128), 0)
    col = lax.broadcasted_iota(jnp.int32, (256, 128), 1)
    same = ((row & 127) >> 6) == (col >> 6)
    return jnp.where(same, 1.0 / HEAD_DIM, 0.0).astype(BF)


def qkv_kernel(begin, sources, parts, *refs):
    mods, gains, x0, x1, x2, x3, wimg_ref, wtxt_ref = refs[:8]
    outs, (raw_ref, acts_ref) = refs[8:-2], refs[-2:]
    blk = lax.axis_index("blk")
    part = x0.shape[2]
    image_rows = x0.shape[1] - TXT_PAD
    img, txt = sources * image_rows, sources * TXT_PAD
    for j, (ref, first) in enumerate(zip((x0, x1, x2, x3), begin)):
        cols = pl.ds(pl.multiple_of((blk ^ j) * part, part), part)
        raw_ref[:img, cols] = ref[first : first + sources, :image_rows, :].reshape(img, part)
        text = ref[first : first + sources, image_rows:, :].astype(F32).reshape(txt, part)
        raw_ref[img:, cols] = text.astype(BF)
    norm_rows(raw_ref, acts_ref, img, txt, mods[8:9, :], mods[9:10, :])
    norm_rows(raw_ref, acts_ref, 0, img, mods[0:1, :], mods[1:2, :])
    group = group_matrix()
    kv_ref = outs[-1]
    for w_ref, first, last, row in ((wtxt_ref, img, img + txt, 2), (wimg_ref, 0, img, 0)):
        projected = dot(acts_ref[first:last, :], w_ref[:, : len(parts) * part])
        for i, which in enumerate(parts):
            values = projected[:, i * part : (i + 1) * part]
            if which == 2:
                kv_ref[1, first:last, :] = values.astype(BF)
                continue
            gain = jnp.concatenate([gains[row + which : row + which + 1, :]] * (part // 128), axis=1)
            normed = (values * head_scale(values, group) * gain).astype(BF)
            if which == 1:
                kv_ref[0, first:last, :] = normed
            else:
                outs[0][first:last, :] = normed * BF(HEAD_DIM**-0.5)


def qkv_call(mods, gains, pieces, begin, sources, weights, parts):
    part = pieces[0].shape[2]
    rows, width = sources * pieces[0].shape[1], 4 * part
    outs = [jax.ShapeDtypeStruct((2, rows, part), BF)]
    if 0 in parts:
        outs = [jax.ShapeDtypeStruct((rows, part), BF)] + outs
    return pl.pallas_call(
        functools.partial(qkv_kernel, begin, sources, parts),
        out_shape=outs,
        in_specs=[VM] * 8,
        out_specs=[VM] * len(outs),
        scratch_shapes=[pltpu.VMEM((rows, width), BF)] * 2,
        compiler_params=pltpu.CompilerParams(vmem_limit_bytes=VMEM_LIMIT),
        cost_estimate=COST,
        name="qkv",
    )(mods, gains, *pieces, *weights)


def head_scores(query, keys, lane, one_lane, head):
    mine = (lane < 64) if head == 0 else (lane >= 64)
    left = jnp.concatenate([jnp.where(mine, query, BF(0.0)), one_lane], axis=1)
    return [dot_t(left, key) for key in keys]


def both_halves(values, lane):
    return jnp.where(lane < 64, values[0], values[1])


def lane_masks(rows):
    lane = lax.broadcasted_iota(jnp.int32, (rows, 128), 1)
    return lane, jnp.where(lane == 0, 1.0, 0.0).astype(BF)


def hiding(bias, img_rows):
    return jnp.concatenate([jnp.zeros((img_rows, 128), BF), bias], axis=0)


def biased(ref, bias, cols):
    return jnp.concatenate([ref[0, :, cols], bias], axis=1)


def summed(ref, cols):
    return jnp.concatenate([ref[1, :, cols], jnp.ones((ref.shape[1], 128), BF)], axis=1)


def own_kernel(bias_ref, q_ref, kv_ref, top_ref, sum_ref, out_ref):
    rows, part = q_ref.shape
    count = rows // 2
    bias = hiding(bias_ref[0], rows - bias_ref.shape[1])
    lane, one_lane = lane_masks(count)
    for col in range(0, part, 128):
        cols = slice(col, col + 128)
        key, value = biased(kv_ref, bias, cols), summed(kv_ref, cols)
        for start in range(0, rows, count):
            span = slice(start, start + count)
            tops, sums, outs = [], [], []
            for head in range(2):
                score = head_scores(q_ref[span, cols], [key], lane, one_lane, head)[0]
                top = jnp.max(score, axis=-1, keepdims=True)
                both = dot(jnp.exp(score - top).astype(BF), value)
                tops.append(top)
                outs.append(both[:, :128])
                sums.append(both[:, 128:])
            top_ref[span, cols] = both_halves(tops, lane)
            sum_ref[span, cols] = both_halves(sums, lane)
            out_ref[span, cols] = both_halves(outs, lane)


def own_call(bias, query, keys):
    shape = jax.ShapeDtypeStruct(query.shape, F32)
    return pl.pallas_call(
        own_kernel,
        out_shape=[shape] * 3,
        in_specs=[VM] * 3,
        out_specs=[VM] * 3,
        compiler_params=pltpu.CompilerParams(vmem_limit_bytes=VMEM_LIMIT),
        cost_estimate=COST,
        name="attend_own",
    )(bias, query, keys)


def attend_kernel(start, counts, gate_rows, *refs):
    groups = len(counts)
    count = sum(counts)
    mods, bias_ref, q_ref, top_ref, sum_ref, out_ref, kv_ref = refs[:7]
    w_refs = refs[7 : 7 + groups]
    part = q_ref.shape[1]
    lane, one_lane = lane_masks(count)
    bias = hiding(bias_ref[1], kv_ref.shape[1] - bias_ref.shape[1])
    span = slice(start, start + count)
    att = []
    for col in range(0, part, 128):
        cols = slice(col, col + 128)
        key, val = biased(kv_ref, bias, cols), summed(kv_ref, cols)
        outs, sums, scales = [], [], []
        for head in range(2):
            score = head_scores(q_ref[span, cols], [key], lane, one_lane, head)[0]
            before = top_ref[span, col + 64 * head : col + 64 * head + 1]
            top = jnp.maximum(before, jnp.max(score, axis=-1, keepdims=True))
            both = dot(jnp.exp(score - top).astype(BF), val)
            outs.append(both[:, :128])
            sums.append(both[:, 128:])
            scales.append(jnp.exp(before - top))
        scale = both_halves(scales, lane)
        total = both_halves(sums, lane) + scale * sum_ref[span, cols]
        att.append(((both_halves(outs, lane) + scale * out_ref[span, cols]) / total).astype(BF))
    att = jnp.concatenate(att, axis=1)
    first = 0
    for i, (rows, row) in enumerate(zip(counts, gate_rows)):
        outs = refs[7 + groups + 2 * i : 9 + groups + 2 * i]
        keep_ref, send_ref = outs
        sends = (send_ref.at[0], send_ref.at[1])
        project_out(att[first : first + rows], mods[row : row + 1, :], w_refs[i], keep_ref, sends)
        first += rows


def project_out(left, gate, w_ref, keep_ref, sends):
    blk = lax.axis_index("blk")
    part = keep_ref.shape[2]
    width = gate.shape[1]
    for pair in range(2):
        which = (blk >> 1) ^ pair
        value = dot(left, w_ref[:, pl.ds(pl.multiple_of(which * 2 * part, 2 * part), 2 * part)])
        value = value * jnp.where(which == 0, gate[:, : width // 2], gate[:, width // 2 :])
        low, high = value[:, :part].astype(BF), value[:, part:].astype(BF)

        @pl.when((blk & 1) == 0)
        def _():
            keep_ref[pair] = low
            sends[pair][...] = high

        @pl.when((blk & 1) == 1)
        def _():
            keep_ref[pair] = high
            sends[pair][...] = low


def attend_call(mods, bias, query, state, keys, start, counts, gate_rows, weights):
    shapes = []
    for count in counts:
        shapes += [jax.ShapeDtypeStruct((2, count, query.shape[1]), BF)] * 2
    return pl.pallas_call(
        functools.partial(attend_kernel, start, counts, gate_rows),
        out_shape=shapes,
        in_specs=[VM] * (7 + len(weights)),
        out_specs=[VM] * len(shapes),
        compiler_params=pltpu.CompilerParams(vmem_limit_bytes=VMEM_LIMIT),
        cost_estimate=COST,
        name="attend",
    )(mods, bias, query, *state, keys, *weights)


def mlp_kernel(mods, m0, m1, n0, n1, up_ref, down_ref, keep_ref, s0, s1, raw_ref, acts_ref):
    blk = lax.axis_index("blk")
    rows, part = m0.shape
    span = up_ref.shape[1] // 3
    for j in range(4):
        value = (m0, n0, m1, n1)[j][...]
        raw_ref[:, pl.ds(pl.multiple_of((blk ^ j) * part, part), part)] = value
    norm_rows(raw_ref, acts_ref, 0, rows, mods[3:4, :], mods[4:5, :])
    for i in range(3):
        cols = slice(i * span, i * span + span)
        hidden = dot(acts_ref[...], up_ref[:, cols])
        raw_ref[:, cols] = jax.nn.gelu(hidden, approximate=True).astype(BF)
    project_out(raw_ref[...], mods[5:6, :], down_ref, keep_ref, (s0, s1))


def mlp_call(mods, mine, near, up, down):
    rows, part = mine[0].shape
    kept = jax.ShapeDtypeStruct((2, rows, part), BF)
    sent = jax.ShapeDtypeStruct((rows, part), BF)
    return pl.pallas_call(
        mlp_kernel,
        out_shape=[kept, sent, sent],
        in_specs=[VM] * 7,
        out_specs=[VM] * 3,
        scratch_shapes=[pltpu.VMEM((rows, 4 * part), BF)] * 2,
        compiler_params=pltpu.CompilerParams(vmem_limit_bytes=VMEM_LIMIT),
        cost_estimate=COST,
        name="mlp",
    )(mods, *mine, *near, up, down)


def swap(values, axis, size, bit):
    return lax.ppermute(values, axis, [(i, i ^ bit) for i in range(size)])


def after(value, *others):
    return lax.optimization_barrier((value, *others))[0]


def add(*terms):
    return sum(term.astype(F32) for term in terms).astype(BF)


def small_call(kernel, name, outs, args, scratch=(), spec=VM):
    return pl.pallas_call(
        kernel,
        out_shape=[jax.ShapeDtypeStruct(shape, BF) for shape in outs],
        in_specs=[spec] * len(args),
        out_specs=[VM] * len(outs),
        scratch_shapes=list(scratch),
        compiler_params=pltpu.CompilerParams(vmem_limit_bytes=VMEM_LIMIT),
        cost_estimate=COST,
        name=name,
    )(*args)


def pack_kernel(image, text, out_ref, slots_ref, text_ref, sems):
    requests, image_rows, part = image.shape
    copies = fetch((text, image), (text_ref, out_ref.at[:, :image_rows, :]), sems)
    copies[0].wait()
    slots_ref[...] = jnp.zeros_like(slots_ref)
    for slot in range(text_ref.shape[0]):
        value = text_ref[slot].astype(F32)
        for i in range(part // 128):
            slots_ref[i, pl.ds(slot, requests, stride=TXT_PAD), :] = value[:, i * 128 : i * 128 + 128]
    for i in range(part // 128):
        piece = slots_ref[i, : requests * TXT_PAD, :].reshape(requests, TXT_PAD, 128).astype(BF)
        out_ref[:, image_rows:, i * 128 : i * 128 + 128] = piece
    copies[1].wait()


def sum_kernel(left_ref, right_ref, out_ref):
    for i in range(2):
        out_ref[i] = add(left_ref[i], right_ref[i])


def joint_kernel(left_ref, right_ref, text_ref, came_t, image_ref, out_ref):
    rows = image_ref.shape[1]
    text = add(text_ref[1], came_t[1])
    half = text.shape[0] // 2
    for i in range(2):
        value = add(left_ref[i], right_ref[i])
        image_ref[i] = value
        out_ref[i, :rows, :] = value
        out_ref[i, rows:, :] = text[i * half : i * half + half]


def middle_kernel(begin, own_ref, far_ref, sum_ref, back_ref, *outs):
    rows, part = sum_ref.shape[1:]
    image_rows = own_ref.shape[1] - TXT_PAD
    for i, (ref, out_ref) in enumerate(zip((own_ref, far_ref), outs)):
        start = ref[begin : begin + rows // image_rows, :image_rows, :].reshape(rows, part)
        out_ref[...] = add(start, sum_ref[i], back_ref[1 - i, :rows, :])


def away_kernel(keep_ref, came_ref, out_ref):
    out_ref[...] = add(keep_ref[1], came_ref[...])


def unpack_kernel(rows_ref, image_ref, text_ref, slots_ref, order_ref, sems):
    sources, slots, part = rows_ref.shape
    image_rows = slots - TXT_PAD
    image_copy = pltpu.make_async_copy(rows_ref.at[:, :image_rows, :], image_ref, sems.at[0])
    image_copy.start()
    for i in range(part // 128):
        cols = slice(i * 128, i * 128 + 128)
        value = rows_ref[:, image_rows:, cols].astype(F32)
        slots_ref[i, : sources * TXT_PAD, :] = value.reshape(sources * TXT_PAD, 128)
        for slot in range(order_ref.shape[0]):
            order_ref[slot, :, cols] = slots_ref[i, pl.ds(slot, sources, stride=TXT_PAD), :].astype(BF)
    text_copy = pltpu.make_async_copy(order_ref, text_ref, sems.at[1])
    text_copy.start()
    image_copy.wait()
    text_copy.wait()


def first_kernel(own_ref, keep_t, came_t, back_b, mid_a, keep_a, came_a, last_a, image_ref, text_ref):
    image_ref[...] = add(mid_a[...], keep_a[0], came_a[...], last_a[...])
    sources, slots, part = own_ref.shape
    rows = back_b.shape[1] - keep_t.shape[1] // 2
    back = jnp.concatenate([back_b[0, rows:, :], back_b[1, rows:, :]], axis=0)
    total = keep_t[0].astype(F32) + came_t[0].astype(F32) + back.astype(F32)
    text = own_ref[:, slots - TXT_PAD :, :].astype(F32) + total.reshape(sources, TXT_PAD, part)
    text_ref[...] = text.astype(BF)


def final_kernel(image_ref, text_ref, mid_b, keep_b, came_b, last_b, out_ref):
    sources, slots, part = out_ref.shape
    image_rows = slots - TXT_PAD
    first = image_ref.shape[0] // image_rows
    out_ref[:first, :image_rows, :] = image_ref[...].reshape(first, image_rows, part)
    value = add(mid_b[...], keep_b[0], came_b[...], last_b[...])
    out_ref[first:, :image_rows, :] = value.reshape(sources - first, image_rows, part)
    out_ref[:, image_rows:, :] = text_ref[...]


def per_device(
    tiles,
    image_tokens,
    text_tokens,
    step_index,
    text_length,
    image_table,
    text_table,
    qkv_image,
    qkv_text,
    attn_out_image,
    attn_out_text,
    query_gain_image,
    key_gain_image,
    query_gain_text,
    key_gain_text,
    up_weight,
    down_weight,
):
    requests, image_rows, part = image_tokens.shape
    text_rows = text_tokens.shape[1]
    groups = [[t for t in range(tiles) if (t >> 1) & 1 == p] for p in (0, 1)]
    tables = [jnp.transpose(table, (1, 0, 2)) for table in (image_table, text_table)]
    weights = [jnp.transpose(weight, (1, 0, 2)) for weight in (qkv_image, qkv_text)]
    gains = [
        gain.reshape(1, HEAD_DIM)
        for gain in (query_gain_image, key_gain_image, query_gain_text, key_gain_text)
    ]

    slots = (requests, image_rows + TXT_PAD, part)
    text_slots = jnp.transpose(text_tokens, (1, 0, 2))
    packed = small_call(
        pack_kernel,
        "pack",
        [slots],
        pinned(image_tokens, text_slots),
        [
            pltpu.VMEM((part // 128, (requests + 1) * TXT_PAD, 128), F32),
            pltpu.VMEM(text_slots.shape, BF),
            pltpu.SemaphoreType.DMA((2,)),
        ],
        HB,
    )[0]
    own = lax.all_to_all(packed, "tile", 0, 0, axis_index_groups=groups, tiled=True)
    far = swap(own, "blk", 4, 2)
    other = swap(own, "tile", tiles, 2)
    own_near = swap(own, "blk", 4, 1)
    mods, head_gains, bias, *wide = prep_call(after(step_index, own), text_length, tables, gains, weights)

    def tied(*others):
        return after(mods, *others)

    def project(mods, pieces, parts):
        return qkv_call(mods, head_gains, pieces, (0, 0, 0, 0), requests, wide, parts)

    far = after(far, mods)
    other = after(other, far)
    other_far = swap(other, "blk", 4, 2)
    diag = swap(far, "blk", 4, 1)
    query, mine = project(mods, [own, own_near, far, diag], PARTS)
    other_near = swap(after(other, query), "blk", 4, 1)
    state = own_call(bias, query, mine)
    other_far = after(other_far, state[0])
    other_diag = swap(other_far, "blk", 4, 1)
    keys = project(tied(state[0]), [other, other_near, other_far, other_diag], PARTS[:2])[0]

    first = requests * 10 // 16
    rows_a, rows_b = first * image_rows, (requests - first) * image_rows
    txt_rows = requests * TXT_PAD

    def attend(mods, *groups):
        return attend_call(mods, bias, query, state, keys, *groups)

    def middle(begin, sums, back):
        kernel = functools.partial(middle_kernel, begin)
        return small_call(kernel, "middle", [sums.shape[1:]] * 2, [own, far, sums, back])

    def near(value):
        return swap(value, "blk", 4, 1)

    def across(value):
        return swap(value, "blk", 4, 2)

    def away(kept, came):
        return small_call(away_kernel, "away", [came.shape], [kept, came])[0]

    keep_a, send_a = attend(mods, 0, (rows_a,), (2,), (attn_out_image,))
    sum_a = small_call(sum_kernel, "core_sum", [keep_a.shape], [keep_a, near(send_a)])[0]
    back_a = across(sum_a)
    keep_b, send_b, keep_t, send_t = attend(
        tied(sum_a), rows_a, (rows_b, txt_rows), (2, 10), (attn_out_image, attn_out_text)
    )
    came_t = near(send_t)
    shapes = [keep_b.shape, (2, rows_b + txt_rows // 2, part)]
    sum_b, joint = small_call(joint_kernel, "joint", shapes, [keep_b, near(send_b), keep_t, came_t])
    back_b = across(joint)
    mid_a = middle(0, sum_a, after(back_a, sum_b))
    near_a = [near(value) for value in mid_a]

    down_a, *send_a = mlp_call(mods, mid_a, near_a, up_weight, down_weight)
    came_a = [near(value) for value in send_a]
    mid_b = middle(first, sum_b, after(back_b, down_a))
    near_b = [near(value) for value in mid_b]
    away_a = away(after(down_a, *near_b), came_a[1])
    last_a = across(away_a)
    down_b, *send_b = mlp_call(tied(away_a), mid_b, near_b, up_weight, down_weight)
    args = [own, keep_t, came_t, back_b, mid_a[0], down_a, came_a[0], after(last_a, down_b)]
    image_a, text_out = small_call(
        first_kernel, "first", [(rows_a, part), (requests, TXT_PAD, part)], args
    )
    came_b = [near(value) for value in send_b]
    away_b = away(after(down_b, image_a), came_b[1])
    last_b = across(away_b)

    args = [image_a, text_out, mid_b[0], down_b, came_b[0], last_b]
    result = small_call(final_kernel, "final", [slots], args)[0]
    result = lax.all_to_all(result, "tile", 0, 0, axis_index_groups=groups, tiled=True)
    shapes = [image_tokens.shape, text_slots.shape]
    image_out, text_out = pl.pallas_call(
        unpack_kernel,
        out_shape=[jax.ShapeDtypeStruct(shape, BF) for shape in shapes],
        in_specs=[VM],
        out_specs=[HB] * 2,
        scratch_shapes=[
            pltpu.VMEM((part // 128, (requests + 1) * TXT_PAD, 128), F32),
            pltpu.VMEM(text_slots.shape, BF),
            pltpu.SemaphoreType.DMA((2,)),
        ],
        compiler_params=pltpu.CompilerParams(vmem_limit_bytes=VMEM_LIMIT),
        cost_estimate=COST,
        name="unpack",
    )(result)
    return (image_out, jnp.transpose(text_out, (1, 0, 2)))


def solution(mesh):
    in_specs = (
        P(None, "tile", "blk"),
        P(None, "tile", "blk"),
        P(),
        P(),
        P(),
        P(),
        P(None, None, "blk"),
        P(None, None, "blk"),
        P("blk", None),
        P("blk", None),
        P(),
        P(),
        P(),
        P(),
        P(None, "blk"),
        P("blk", None),
    )
    out_specs = (P(None, "tile", "blk"), P(None, "tile", "blk"))
    return jax.shard_map(
        functools.partial(per_device, mesh.shape["tile"]),
        mesh=mesh,
        in_specs=in_specs,
        out_specs=out_specs,
        check_vma=False,
    )
```

```python
import functools

import jax
import jax.numpy as jnp
from jax import lax
from jax.experimental import pallas as pl
from jax.experimental.pallas import tpu as pltpu
from jax.sharding import PartitionSpec as P

HEAD_DIM = 64
BF = jnp.bfloat16
F32 = jnp.float32
QUERY_SCALE = HEAD_DIM**-0.5 * 1.4426950408889634
HIDDEN_BIAS = -32768.0
TXT_PAD = 8
PARTS = (1, 2, 0)
VMEM_LIMIT = 28 << 20
VM = pl.BlockSpec(memory_space=pltpu.VMEM)
SM = pl.BlockSpec(memory_space=pltpu.SMEM)
HB = pl.BlockSpec(memory_space=pltpu.HBM)
COST = pl.CostEstimate(flops=1, transcendentals=0, bytes_accessed=1)


def dot(left, right):
    return jnp.dot(left, right, preferred_element_type=F32)


def dot_t(left, right):
    return lax.dot_general(left, right, (((1,), (1,)), ((), ())), preferred_element_type=F32)


def pinned(*arrays):
    return [pltpu.with_memory_space_constraint(array, pltpu.HBM) for array in arrays]


def fetch(sources, targets, sems):
    copies = [
        pltpu.make_async_copy(source, target, sems.at[i])
        for i, (source, target) in enumerate(zip(sources, targets))
    ]
    for copy in copies:
        copy.start()
    return copies


def table_row(table_ref, step, row):
    plane = table_ref[row].astype(F32)
    here = lax.broadcasted_iota(jnp.int32, plane.shape, 0) == step
    return jnp.sum(jnp.where(here, plane, 0.0), axis=0, keepdims=True)


def prep_kernel(step_ref, length_ref, *refs):
    mods_ref, gains_ref, bias_ref, wimg_ref, wtxt_ref = refs[8:13]
    part = refs[6].shape[2]
    sources, targets = list(refs[:6]), list(refs[13:19])
    for w, w_ref in zip(refs[6:8], (wimg_ref, wtxt_ref)):
        for i, which in enumerate(PARTS):
            sources.append(w.at[which])
            targets.append(w_ref.at[:, i * part : (i + 1) * part])
    copies = fetch(sources, targets, refs[19])
    for copy in copies[:6]:
        copy.wait()
    itab, ttab, gqi, gki, gqt, gkt = refs[13:19]
    tile = lax.axis_index("tile")
    request = (tile >> 2) * 2 + (tile & 1)
    step, length = step_ref[request], length_ref[request]
    for row in range(6):
        mods_ref[row : row + 1, :] = table_row(itab, step, row)
    for row in range(3):
        mods_ref[8 + row : 9 + row, :] = table_row(ttab, step, row)
    for row, ref in enumerate((gqi, gki, gqt, gkt)):
        gains_ref[row : row + 1, :] = jnp.concatenate([ref[...], ref[...]], axis=1)
    inner = lax.broadcasted_iota(jnp.int32, bias_ref.shape[1:], 0)
    source, slot = inner >> 3, inner & 7
    for side in range(2):
        parity = ((tile >> 1) & 1) ^ side
        sender = (source >> 1) * 4 + parity * 2 + (source & 1)
        seen = (slot < 5) & (sender * 5 + slot < length)
        bias_ref[side] = jnp.where(seen, 0.0, HIDDEN_BIAS).astype(BF)
    for copy in copies[6:]:
        copy.wait()


def prep_call(step_index, text_length, tables, gains, weights):
    width = tables[0].shape[2]
    wide = jax.ShapeDtypeStruct((width, 3 * weights[0].shape[2]), BF)
    return pl.pallas_call(
        prep_kernel,
        out_shape=[
            jax.ShapeDtypeStruct((16, width), F32),
            jax.ShapeDtypeStruct((8, 128), F32),
            jax.ShapeDtypeStruct((2, 128, 128), BF),
            wide,
            wide,
        ],
        in_specs=[SM, SM] + [HB] * 8,
        out_specs=[VM] * 5,
        scratch_shapes=[pltpu.VMEM(x.shape, x.dtype) for x in (*tables, *gains)]
        + [pltpu.SemaphoreType.DMA((12,))],
        compiler_params=pltpu.CompilerParams(vmem_limit_bytes=VMEM_LIMIT),
        cost_estimate=COST,
        name="prep",
    )(step_index, text_length, *pinned(*tables, *gains, *weights))


def norm_rows(raw_ref, acts_ref, start, count, shift, scale, block=32):
    width = raw_ref.shape[1]
    gain = 1.0 + scale

    def body(i, carry):
        rows = pl.ds(pl.multiple_of(start + i * block, block), block)
        values = raw_ref[rows, :].astype(F32)
        centre = jnp.sum(values, axis=-1, keepdims=True) * (1.0 / width)
        moved = values - centre
        spread = jnp.sum(moved * moved, axis=-1, keepdims=True) * (1.0 / width)
        acts_ref[rows, :] = (moved * lax.rsqrt(spread + 1e-06) * gain + shift).astype(BF)
        return carry

    lax.fori_loop(0, count // block, body, 0, unroll=True)


def head_scale(values, group):
    parts = []
    for col in range(0, values.shape[1], 128):
        piece = values[:, col : col + 128]
        squares = piece * piece
        high = squares.astype(BF)
        low = (squares - high.astype(F32)).astype(BF)
        parts.append(dot(jnp.concatenate([high, low], axis=1), group))
    return lax.rsqrt(jnp.concatenate(parts, axis=1) + 1e-06)


def group_matrix():
    row = lax.broadcasted_iota(jnp.int32, (256, 128), 0)
    col = lax.broadcasted_iota(jnp.int32, (256, 128), 1)
    same = ((row & 127) >> 6) == (col >> 6)
    return jnp.where(same, 1.0 / HEAD_DIM, 0.0).astype(BF)


def qkv_kernel(begin, sources, parts, *refs):
    mods, gains, x0, x1, x2, x3, wimg_ref, wtxt_ref = refs[:8]
    outs, (raw_ref, acts_ref) = refs[8:-2], refs[-2:]
    blk = lax.axis_index("blk")
    part = x0.shape[2]
    image_rows = x0.shape[1] - TXT_PAD
    img, txt = sources * image_rows, sources * TXT_PAD
    for j, (ref, first) in enumerate(zip((x0, x1, x2, x3), begin)):
        cols = pl.ds(pl.multiple_of((blk ^ j) * part, part), part)
        raw_ref[:img, cols] = ref[first : first + sources, :image_rows, :].reshape(img, part)
        text = ref[first : first + sources, image_rows:, :].astype(F32).reshape(txt, part)
        raw_ref[img:, cols] = text.astype(BF)
    norm_rows(raw_ref, acts_ref, img, txt, mods[8:9, :], mods[9:10, :])
    norm_rows(raw_ref, acts_ref, 0, img, mods[0:1, :], mods[1:2, :])
    group = group_matrix()
    kv_ref = outs[-1]
    for w_ref, first, last, row in ((wtxt_ref, img, img + txt, 2), (wimg_ref, 0, img, 0)):
        projected = dot(acts_ref[first:last, :], w_ref[:, : len(parts) * part])
        for i, which in enumerate(parts):
            values = projected[:, i * part : (i + 1) * part]
            if which == 2:
                kv_ref[1, first:last, :] = values.astype(BF)
                continue
            gain = jnp.concatenate([gains[row + which : row + which + 1, :]] * (part // 128), axis=1)
            normed = values * head_scale(values, group) * gain
            if which == 1:
                kv_ref[0, first:last, :] = normed.astype(BF)
            else:
                outs[0][first:last, :] = (normed * QUERY_SCALE).astype(BF)


def qkv_call(mods, gains, pieces, begin, sources, weights, parts):
    part = pieces[0].shape[2]
    rows, width = sources * pieces[0].shape[1], 4 * part
    outs = [jax.ShapeDtypeStruct((2, rows, part), BF)]
    if 0 in parts:
        outs = [jax.ShapeDtypeStruct((rows, part), BF)] + outs
    return pl.pallas_call(
        functools.partial(qkv_kernel, begin, sources, parts),
        out_shape=outs,
        in_specs=[VM] * 8,
        out_specs=[VM] * len(outs),
        scratch_shapes=[pltpu.VMEM((rows, width), BF)] * 2,
        compiler_params=pltpu.CompilerParams(vmem_limit_bytes=VMEM_LIMIT),
        cost_estimate=COST,
        name="qkv",
    )(mods, gains, *pieces, *weights)


def head_scores(query, keys, lane, one_lane, head):
    mine = (lane < 64) if head == 0 else (lane >= 64)
    left = jnp.concatenate([jnp.where(mine, query, BF(0.0)), one_lane], axis=1)
    return [dot_t(left, key) for key in keys]


def both_halves(values, lane):
    return jnp.where(lane < 64, values[0], values[1])


def lane_masks(rows):
    lane = lax.broadcasted_iota(jnp.int32, (rows, 128), 1)
    return lane, jnp.where(lane == 0, 1.0, 0.0).astype(BF)


def hiding(bias, img_rows):
    return jnp.concatenate([jnp.zeros((img_rows, 128), BF), bias], axis=0)


def biased(ref, bias, cols):
    return jnp.concatenate([ref[0, :, cols], bias], axis=1)


def summed(ref, cols):
    return jnp.concatenate([ref[1, :, cols], jnp.ones((ref.shape[1], 128), BF)], axis=1)


def own_kernel(bias_ref, q_ref, kv_ref, top_ref, sum_ref, out_ref):
    rows, part = q_ref.shape
    count = rows // 2
    bias = hiding(bias_ref[0], rows - bias_ref.shape[1])
    lane, one_lane = lane_masks(count)
    for col in range(0, part, 128):
        cols = slice(col, col + 128)
        key, value = biased(kv_ref, bias, cols), summed(kv_ref, cols)
        for start in range(0, rows, count):
            span = slice(start, start + count)
            tops, sums, outs = [], [], []
            for head in range(2):
                score = head_scores(q_ref[span, cols], [key], lane, one_lane, head)[0]
                top = jnp.max(score, axis=-1, keepdims=True)
                both = dot(jnp.exp2(score - top).astype(BF), value)
                tops.append(top)
                outs.append(both[:, :128])
                sums.append(both[:, 128:])
            top_ref[span, cols] = both_halves(tops, lane)
            sum_ref[span, cols] = both_halves(sums, lane)
            out_ref[span, cols] = both_halves(outs, lane)


def own_call(bias, query, keys):
    shape = jax.ShapeDtypeStruct(query.shape, F32)
    return pl.pallas_call(
        own_kernel,
        out_shape=[shape] * 3,
        in_specs=[VM] * 3,
        out_specs=[VM] * 3,
        compiler_params=pltpu.CompilerParams(vmem_limit_bytes=VMEM_LIMIT),
        cost_estimate=COST,
        name="attend_own",
    )(bias, query, keys)


def attend_kernel(start, counts, gate_rows, *refs):
    groups = len(counts)
    count = sum(counts)
    mods, bias_ref, q_ref, top_ref, sum_ref, out_ref, kv_ref = refs[:7]
    w_refs = refs[7 : 7 + groups]
    part = q_ref.shape[1]
    lane, one_lane = lane_masks(count)
    bias = hiding(bias_ref[1], kv_ref.shape[1] - bias_ref.shape[1])
    span = slice(start, start + count)
    att = []
    for col in range(0, part, 128):
        cols = slice(col, col + 128)
        key, val = biased(kv_ref, bias, cols), summed(kv_ref, cols)
        outs, sums, scales = [], [], []
        for head in range(2):
            score = head_scores(q_ref[span, cols], [key], lane, one_lane, head)[0]
            before = top_ref[span, col + 64 * head : col + 64 * head + 1]
            top = jnp.maximum(before, jnp.max(score, axis=-1, keepdims=True))
            both = dot(jnp.exp2(score - top).astype(BF), val)
            outs.append(both[:, :128])
            sums.append(both[:, 128:])
            scales.append(jnp.exp2(before - top))
        scale = both_halves(scales, lane)
        total = both_halves(sums, lane) + scale * sum_ref[span, cols]
        att.append(((both_halves(outs, lane) + scale * out_ref[span, cols]) / total).astype(BF))
    att = jnp.concatenate(att, axis=1)
    first = 0
    for i, (rows, row) in enumerate(zip(counts, gate_rows)):
        outs = refs[7 + groups + 2 * i : 9 + groups + 2 * i]
        keep_ref, send_ref = outs
        sends = (send_ref.at[0], send_ref.at[1])
        project_out(att[first : first + rows], mods[row : row + 1, :], w_refs[i], keep_ref, sends)
        first += rows


def project_out(left, gate, w_ref, keep_ref, sends):
    blk = lax.axis_index("blk")
    part = keep_ref.shape[2]
    width = gate.shape[1]
    for pair in range(2):
        which = (blk >> 1) ^ pair
        value = dot(left, w_ref[:, pl.ds(pl.multiple_of(which * 2 * part, 2 * part), 2 * part)])
        value = value * jnp.where(which == 0, gate[:, : width // 2], gate[:, width // 2 :])
        low, high = value[:, :part].astype(BF), value[:, part:].astype(BF)

        @pl.when((blk & 1) == 0)
        def _():
            keep_ref[pair] = low
            sends[pair][...] = high

        @pl.when((blk & 1) == 1)
        def _():
            keep_ref[pair] = high
            sends[pair][...] = low


def attend_call(mods, bias, query, state, keys, start, counts, gate_rows, weights):
    shapes = []
    for count in counts:
        shapes += [jax.ShapeDtypeStruct((2, count, query.shape[1]), BF)] * 2
    return pl.pallas_call(
        functools.partial(attend_kernel, start, counts, gate_rows),
        out_shape=shapes,
        in_specs=[VM] * (7 + len(weights)),
        out_specs=[VM] * len(shapes),
        compiler_params=pltpu.CompilerParams(vmem_limit_bytes=VMEM_LIMIT),
        cost_estimate=COST,
        name="attend",
    )(mods, bias, query, *state, keys, *weights)


def mlp_kernel(mods, m0, m1, n0, n1, up_ref, down_ref, keep_ref, s0, s1, raw_ref, acts_ref):
    blk = lax.axis_index("blk")
    rows, part = m0.shape
    span = up_ref.shape[1] // 3
    for j in range(4):
        value = (m0, n0, m1, n1)[j][...]
        raw_ref[:, pl.ds(pl.multiple_of((blk ^ j) * part, part), part)] = value
    norm_rows(raw_ref, acts_ref, 0, rows, mods[3:4, :], mods[4:5, :])
    for i in range(3):
        cols = slice(i * span, i * span + span)
        hidden = dot(acts_ref[...], up_ref[:, cols])
        raw_ref[:, cols] = jax.nn.gelu(hidden, approximate=True).astype(BF)
    project_out(raw_ref[...], mods[5:6, :], down_ref, keep_ref, (s0, s1))


def mlp_call(mods, mine, near, up, down):
    rows, part = mine[0].shape
    kept = jax.ShapeDtypeStruct((2, rows, part), BF)
    sent = jax.ShapeDtypeStruct((rows, part), BF)
    return pl.pallas_call(
        mlp_kernel,
        out_shape=[kept, sent, sent],
        in_specs=[VM] * 7,
        out_specs=[VM] * 3,
        scratch_shapes=[pltpu.VMEM((rows, 4 * part), BF)] * 2,
        compiler_params=pltpu.CompilerParams(vmem_limit_bytes=VMEM_LIMIT),
        cost_estimate=COST,
        name="mlp",
    )(mods, *mine, *near, up, down)


def swap(values, axis, size, bit):
    return lax.ppermute(values, axis, [(i, i ^ bit) for i in range(size)])


def after(value, *others):
    return lax.optimization_barrier((value, *others))[0]


def add(*terms):
    return sum(term.astype(F32) for term in terms).astype(BF)


def small_call(kernel, name, outs, args, scratch=(), spec=VM):
    return pl.pallas_call(
        kernel,
        out_shape=[jax.ShapeDtypeStruct(shape, BF) for shape in outs],
        in_specs=[spec] * len(args),
        out_specs=[VM] * len(outs),
        scratch_shapes=list(scratch),
        compiler_params=pltpu.CompilerParams(vmem_limit_bytes=VMEM_LIMIT),
        cost_estimate=COST,
        name=name,
    )(*args)


def pack_kernel(image, text, out_ref, slots_ref, text_ref, sems):
    requests, image_rows, part = image.shape
    copies = fetch((text, image), (text_ref, out_ref.at[:, :image_rows, :]), sems)
    copies[0].wait()
    slots_ref[...] = jnp.zeros_like(slots_ref)
    for slot in range(text_ref.shape[0]):
        value = text_ref[slot].astype(F32)
        for i in range(part // 128):
            slots_ref[i, pl.ds(slot, requests, stride=TXT_PAD), :] = value[:, i * 128 : i * 128 + 128]
    for i in range(part // 128):
        piece = slots_ref[i, : requests * TXT_PAD, :].reshape(requests, TXT_PAD, 128).astype(BF)
        out_ref[:, image_rows:, i * 128 : i * 128 + 128] = piece
    copies[1].wait()


def sum_kernel(left_ref, right_ref, out_ref):
    for i in range(2):
        out_ref[i] = add(left_ref[i], right_ref[i])


def joint_kernel(left_ref, right_ref, text_ref, came_t, image_ref, out_ref):
    rows = image_ref.shape[1]
    text = add(text_ref[1], came_t[1])
    half = text.shape[0] // 2
    for i in range(2):
        value = add(left_ref[i], right_ref[i])
        image_ref[i] = value
        out_ref[i, :rows, :] = value
        out_ref[i, rows:, :] = text[i * half : i * half + half]


def middle_kernel(begin, own_ref, far_ref, sum_ref, back_ref, *outs):
    rows, part = sum_ref.shape[1:]
    image_rows = own_ref.shape[1] - TXT_PAD
    for i, (ref, out_ref) in enumerate(zip((own_ref, far_ref), outs)):
        start = ref[begin : begin + rows // image_rows, :image_rows, :].reshape(rows, part)
        out_ref[...] = add(start, sum_ref[i], back_ref[1 - i, :rows, :])


def away_kernel(keep_ref, came_ref, out_ref):
    out_ref[...] = add(keep_ref[1], came_ref[...])


def unpack_kernel(rows_ref, image_ref, text_ref, slots_ref, order_ref, sems):
    sources, slots, part = rows_ref.shape
    image_rows = slots - TXT_PAD
    image_copy = pltpu.make_async_copy(rows_ref.at[:, :image_rows, :], image_ref, sems.at[0])
    image_copy.start()
    for i in range(part // 128):
        cols = slice(i * 128, i * 128 + 128)
        value = rows_ref[:, image_rows:, cols].astype(F32)
        slots_ref[i, : sources * TXT_PAD, :] = value.reshape(sources * TXT_PAD, 128)
        for slot in range(order_ref.shape[0]):
            order_ref[slot, :, cols] = slots_ref[i, pl.ds(slot, sources, stride=TXT_PAD), :].astype(BF)
    text_copy = pltpu.make_async_copy(order_ref, text_ref, sems.at[1])
    text_copy.start()
    image_copy.wait()
    text_copy.wait()


def first_kernel(own_ref, keep_t, came_t, back_b, mid_a, keep_a, came_a, last_a, image_ref, text_ref):
    image_ref[...] = add(mid_a[...], keep_a[0], came_a[...], last_a[...])
    sources, slots, part = own_ref.shape
    rows = back_b.shape[1] - keep_t.shape[1] // 2
    back = jnp.concatenate([back_b[0, rows:, :], back_b[1, rows:, :]], axis=0)
    total = keep_t[0].astype(F32) + came_t[0].astype(F32) + back.astype(F32)
    text = own_ref[:, slots - TXT_PAD :, :].astype(F32) + total.reshape(sources, TXT_PAD, part)
    text_ref[...] = text.astype(BF)


def final_kernel(image_ref, text_ref, mid_b, keep_b, came_b, last_b, out_ref):
    sources, slots, part = out_ref.shape
    image_rows = slots - TXT_PAD
    first = image_ref.shape[0] // image_rows
    out_ref[:first, :image_rows, :] = image_ref[...].reshape(first, image_rows, part)
    value = add(mid_b[...], keep_b[0], came_b[...], last_b[...])
    out_ref[first:, :image_rows, :] = value.reshape(sources - first, image_rows, part)
    out_ref[:, image_rows:, :] = text_ref[...]


def per_device(
    tiles,
    image_tokens,
    text_tokens,
    step_index,
    text_length,
    image_table,
    text_table,
    qkv_image,
    qkv_text,
    attn_out_image,
    attn_out_text,
    query_gain_image,
    key_gain_image,
    query_gain_text,
    key_gain_text,
    up_weight,
    down_weight,
):
    requests, image_rows, part = image_tokens.shape
    text_rows = text_tokens.shape[1]
    groups = [[t for t in range(tiles) if (t >> 1) & 1 == p] for p in (0, 1)]
    tables = [jnp.transpose(table, (1, 0, 2)) for table in (image_table, text_table)]
    weights = [jnp.transpose(weight, (1, 0, 2)) for weight in (qkv_image, qkv_text)]
    gains = [
        gain.reshape(1, HEAD_DIM)
        for gain in (query_gain_image, key_gain_image, query_gain_text, key_gain_text)
    ]

    slots = (requests, image_rows + TXT_PAD, part)
    text_slots = jnp.transpose(text_tokens, (1, 0, 2))
    packed = small_call(
        pack_kernel,
        "pack",
        [slots],
        pinned(image_tokens, text_slots),
        [
            pltpu.VMEM((part // 128, (requests + 1) * TXT_PAD, 128), F32),
            pltpu.VMEM(text_slots.shape, BF),
            pltpu.SemaphoreType.DMA((2,)),
        ],
        HB,
    )[0]
    own = lax.all_to_all(packed, "tile", 0, 0, axis_index_groups=groups, tiled=True)
    far = swap(own, "blk", 4, 2)
    other = swap(own, "tile", tiles, 2)
    own_near = swap(own, "blk", 4, 1)
    mods, head_gains, bias, *wide = prep_call(after(step_index, own), text_length, tables, gains, weights)

    def tied(*others):
        return after(mods, *others)

    def project(mods, pieces, parts):
        return qkv_call(mods, head_gains, pieces, (0, 0, 0, 0), requests, wide, parts)

    far = after(far, mods)
    other = after(other, far)
    other_far = swap(other, "blk", 4, 2)
    diag = swap(far, "blk", 4, 1)
    query, mine = project(mods, [own, own_near, far, diag], PARTS)
    other_near = swap(after(other, query), "blk", 4, 1)
    state = own_call(bias, query, mine)
    other_far = after(other_far, state[0])
    other_diag = swap(other_far, "blk", 4, 1)
    keys = project(tied(state[0]), [other, other_near, other_far, other_diag], PARTS[:2])[0]

    first = requests * 10 // 16
    rows_a, rows_b = first * image_rows, (requests - first) * image_rows
    txt_rows = requests * TXT_PAD

    def attend(mods, *groups):
        return attend_call(mods, bias, query, state, keys, *groups)

    def middle(begin, sums, back):
        kernel = functools.partial(middle_kernel, begin)
        return small_call(kernel, "middle", [sums.shape[1:]] * 2, [own, far, sums, back])

    def near(value):
        return swap(value, "blk", 4, 1)

    def across(value):
        return swap(value, "blk", 4, 2)

    def away(kept, came):
        return small_call(away_kernel, "away", [came.shape], [kept, came])[0]

    keep_a, send_a = attend(mods, 0, (rows_a,), (2,), (attn_out_image,))
    sum_a = small_call(sum_kernel, "core_sum", [keep_a.shape], [keep_a, near(send_a)])[0]
    back_a = across(sum_a)
    keep_b, send_b, keep_t, send_t = attend(
        tied(sum_a), rows_a, (rows_b, txt_rows), (2, 10), (attn_out_image, attn_out_text)
    )
    came_t = near(send_t)
    shapes = [keep_b.shape, (2, rows_b + txt_rows // 2, part)]
    sum_b, joint = small_call(joint_kernel, "joint", shapes, [keep_b, near(send_b), keep_t, came_t])
    back_b = across(joint)
    mid_a = middle(0, sum_a, after(back_a, sum_b))
    near_a = [near(value) for value in mid_a]

    down_a, *send_a = mlp_call(mods, mid_a, near_a, up_weight, down_weight)
    came_a = [near(value) for value in send_a]
    mid_b = middle(first, sum_b, after(back_b, down_a))
    near_b = [near(value) for value in mid_b]
    away_a = away(after(down_a, *near_b), came_a[1])
    last_a = across(away_a)
    down_b, *send_b = mlp_call(tied(away_a), mid_b, near_b, up_weight, down_weight)
    args = [own, keep_t, came_t, back_b, mid_a[0], down_a, came_a[0], after(last_a, down_b)]
    image_a, text_out = small_call(
        first_kernel, "first", [(rows_a, part), (requests, TXT_PAD, part)], args
    )
    came_b = [near(value) for value in send_b]
    away_b = away(after(down_b, image_a), came_b[1])
    last_b = across(away_b)

    args = [image_a, text_out, mid_b[0], down_b, came_b[0], last_b]
    result = small_call(final_kernel, "final", [slots], args)[0]
    result = lax.all_to_all(result, "tile", 0, 0, axis_index_groups=groups, tiled=True)
    shapes = [image_tokens.shape, text_slots.shape]
    image_out, text_out = pl.pallas_call(
        unpack_kernel,
        out_shape=[jax.ShapeDtypeStruct(shape, BF) for shape in shapes],
        in_specs=[VM],
        out_specs=[HB] * 2,
        scratch_shapes=[
            pltpu.VMEM((part // 128, (requests + 1) * TXT_PAD, 128), F32),
            pltpu.VMEM(text_slots.shape, BF),
            pltpu.SemaphoreType.DMA((2,)),
        ],
        compiler_params=pltpu.CompilerParams(vmem_limit_bytes=VMEM_LIMIT),
        cost_estimate=COST,
        name="unpack",
    )(result)
    return (image_out, jnp.transpose(text_out, (1, 0, 2)))


def solution(mesh):
    in_specs = (
        P(None, "tile", "blk"),
        P(None, "tile", "blk"),
        P(),
        P(),
        P(),
        P(),
        P(None, None, "blk"),
        P(None, None, "blk"),
        P("blk", None),
        P("blk", None),
        P(),
        P(),
        P(),
        P(),
        P(None, "blk"),
        P("blk", None),
    )
    out_specs = (P(None, "tile", "blk"), P(None, "tile", "blk"))
    return jax.shard_map(
        functools.partial(per_device, mesh.shape["tile"]),
        mesh=mesh,
        in_specs=in_specs,
        out_specs=out_specs,
        check_vma=False,
    )
```
